128 devices in a mesh: major: 8 (over x_lo, y), minor: 16 (over z, x_hi, core).
Axes of the slice: x: 4 (x_hi: 2, x_lo: 2; x = x_hi * 2 + x_lo), y: 4, z: 4, core: 2. Of those that a mesh axis runs over, the one named last changes fastest.
Arguments:
- block_in: bfloat16 [16384, 1024], P(('major', 'minor')), may hold values from -24 to 24
- out_cot: bfloat16 [16384, 1024], P(('major', 'minor')), may hold values from -6 to 6
- w_in: bfloat16 [1024, 3072], replicated, may hold values from -0.1875 to 0.1875
- w_out: bfloat16 [1024, 1024], replicated, may hold values from -0.1875 to 0.1875
- conv_one: bfloat16 [16384, 1024], P(('major', 'minor')), may hold values from -6 to 6
- conv_two: bfloat16 [16384, 1024], P(('major', 'minor')), may hold values from -6 to 6
- filter_one: bfloat16 [16384, 1024], P(('major', 'minor')), may hold values from -6 to 6
- filter_two: bfloat16 [16384, 1024], P(('major', 'minor')), may hold values from -6 to 6
Outputs:
- in_grad: bfloat16 [16384, 1024], P(('major', 'minor'))
- w_in_grad: float32 [1024, 3072], P(('major', 'minor'))
- w_out_grad: float32 [1024, 1024], P(('major', 'minor'))
- filter_one_grad: bfloat16 [16384, 1024], P(('major', 'minor'))
- filter_two_grad: bfloat16 [16384, 1024], P(('major', 'minor'))
The draws below stay inside these ranges and needn't reach their ends.
All inputs are finite; a program needn't handle non-finite values.
Results may differ from the reference program's by a relative error of at most 0.014.
Values may be sent and summed in bfloat16 or wider, within the bound.
A program may use at most 128 MiB of HBM per device.

```python
import jax
import jax.numpy as jnp

D = 1024
TOKENS = 16384


def with_spikes(array, rng, source, target, parts, factor):
    owner, partner = [(jnp.arange(array.shape[dim]) // (array.shape[dim] // parts)).reshape([-1 if axis == dim else 1 for axis in range(array.ndim)]) for dim in (source, target)]
    chosen = jax.random.permutation(rng, parts)[partner]
    strong = (owner == chosen) | (owner == (partner + parts // 2) % parts)
    return jnp.where(strong, factor * array, array)


def steps_of(key, shape, cuts, low, top_value):
    level = 1.0
    for dim, shards_of in cuts:
        steps = jax.random.uniform(jax.random.fold_in(jax.random.fold_in(key, 6), dim), (shards_of,), jnp.float32, low / len(cuts), top_value / len(cuts))
        level = level * jnp.repeat(jnp.exp(steps), shape[dim] // shards_of).reshape((-1,) + (1,) * (len(shape) - 1 - dim))
    return level


def centred(key, dims, deviation, most, shards=(), kind=jnp.bfloat16):
    entries = jax.random.normal(key, dims, jnp.float32) * deviation
    if len(shards) > 0:
        entries = steps_of(key, dims, shards, -0.22, 0.18) * entries
    return jnp.clip(entries, min=-most, max=most).astype(kind)


def bell_draw_with(own_key, dims, width, reach, split, heavy, kind=jnp.bfloat16):
    result = width * jax.random.normal(own_key, dims, jnp.float32)
    if split:
        result = result * steps_of(own_key, dims, split, -0.22, 0.18)
    return jnp.clip(with_spikes(result, jax.random.fold_in(own_key, 3), *heavy), -reach, reach).astype(kind)


def setup_inputs(seed: int = 0) -> dict:
    key_list = jax.random.split(jax.random.key(seed), 9)
    block_in = bell_draw_with(key_list[0], (TOKENS, D), 1.0, 24.0, ((0, 128),), (0, 1, 128, 5.5))
    out_cot = centred(key_list[1], (TOKENS, D), 1.0, 6.0, ((0, 128),))
    w_in = centred(key_list[2], (D, 3 * D), D ** -0.5, 0.1875)
    w_out = centred(key_list[3], (D, D), D ** -0.5, 0.1875)
    conv_one = centred(key_list[4], (TOKENS, D), 1.0, 6.0, ((0, 128),))
    conv_two = centred(key_list[5], (TOKENS, D), 1.0, 6.0, ((0, 128),))
    filter_one = centred(key_list[6], (TOKENS, D), 1.0, 6.0, ((0, 128),))
    filter_two = centred(key_list[7], (TOKENS, D), 1.0, 6.0, ((0, 128),))
    return {"block_in": block_in, "out_cot": out_cot, "w_in": w_in, "w_out": w_out, "conv_one": conv_one, "conv_two": conv_two, "filter_one": filter_one, "filter_two": filter_two}


def spectrum(field):
    return jnp.fft.rfft(field.astype(jnp.float32), n=2 * TOKENS, axis=0)


def correlate(left_spec, right_spec):
    return jnp.fft.irfft(left_spec * jnp.conj(right_spec), n=2 * TOKENS, axis=0)[:TOKENS]


def product(left, right):
    return (left.astype(jnp.float32) * right.astype(jnp.float32)).astype(jnp.bfloat16)


def reference(block_in, out_cot, w_in, w_out, conv_one, conv_two, filter_one, filter_two):
    scale = TOKENS ** -0.5
    proj = jnp.dot(block_in, w_in, preferred_element_type=jnp.float32).astype(jnp.bfloat16)
    value = proj[:, :D]
    gate_one = proj[:, D:2 * D]
    gate_two = proj[:, 2 * D:]
    first_out = product(gate_one, conv_one)
    second_out = product(gate_two, conv_two)
    grad_second = jnp.dot(out_cot, w_out.T, preferred_element_type=jnp.float32).astype(jnp.bfloat16)
    grad_conv_two = product(grad_second, gate_two)
    grad_gate_two = product(grad_second, conv_two)
    spec_two = spectrum(grad_conv_two)
    grad_first = (correlate(spec_two, spectrum(filter_two)) * scale).astype(jnp.bfloat16)
    filter_two_grad = (correlate(spec_two, spectrum(first_out)) * scale).astype(jnp.bfloat16)
    grad_conv_one = product(grad_first, gate_one)
    grad_gate_one = product(grad_first, conv_one)
    spec_one = spectrum(grad_conv_one)
    grad_value = (correlate(spec_one, spectrum(filter_one)) * scale).astype(jnp.bfloat16)
    filter_one_grad = (correlate(spec_one, spectrum(value)) * scale).astype(jnp.bfloat16)
    grad_proj = jnp.concatenate([grad_value, grad_gate_one, grad_gate_two], axis=1)
    in_grad = jnp.dot(grad_proj, w_in.T, preferred_element_type=jnp.float32).astype(jnp.bfloat16)
    w_in_grad = jnp.dot(block_in.T, grad_proj, preferred_element_type=jnp.float32) * scale
    w_out_grad = jnp.dot(second_out.T, out_cot, preferred_element_type=jnp.float32) * scale
    return in_grad, w_in_grad, w_out_grad, filter_one_grad, filter_two_grad
```

```python
import functools

import jax
import jax.numpy as jnp
import numpy as np
from jax import lax
from jax.experimental import pallas as pl
from jax.experimental.pallas import tpu as pltpu
from jax.sharding import PartitionSpec as P

AXES = ("major", "minor")
DEV = 128
CH = 8
LANES = 128
BF = jnp.bfloat16
F32 = jnp.float32
VALUE, GATE_ONE, CONV_ONE, FILTER_ONE, FILTER_TWO, GRAD_CONV_TWO = range(6)
FIELDS_IN = 6
FIELDS_OUT = 4


def dft_tables():
    k1 = np.arange(256)[:, None]
    n1 = np.arange(128)[None, :]
    a = 2.0 * np.pi * ((k1 * n1) % 256) / 256
    c, s = np.cos(a), np.sin(a)
    n2 = np.arange(128)
    b = 2.0 * np.pi * ((n2[:, None] * n2[None, :]) % 128) / 128
    cb, sb = np.cos(b), np.sin(b)
    t = 2.0 * np.pi * (k1 * n2[None, :]) / 32768
    return (
        np.block([[c, -s], [-s, -c]]).astype(BF),
        np.block([[c.T, -s.T], [s.T, c.T]]).astype(BF),
        np.block([[cb, -sb], [sb, cb]]).astype(BF),
        np.block([[cb, sb], [-sb, cb]]).astype(BF),
        np.stack([np.cos(t), np.sin(t)]).astype(np.float32),
    )


def round_mul(a, b):
    return (a * b).astype(BF).astype(F32)


def spectrum_of(data, table, line, tw_re, tw_im):
    grid = jnp.dot(table, data, preferred_element_type=F32)
    out = []
    for h in range(2):
        re = grid[:256, h * 128 : h * 128 + 128]
        im = grid[256:, h * 128 : h * 128 + 128]
        turned = jnp.concatenate([re * tw_re + im * tw_im, im * tw_re - re * tw_im], axis=1)
        out.append(jnp.dot(turned.astype(BF), line, preferred_element_type=F32))
    return out


def correlations(left, pair, refs, factor):
    fwd, inv, line, line_back, turn = refs
    tw_re, tw_im = turn[0], turn[1]
    specs = spectrum_of(left.astype(BF), fwd[:, :128], line[...], tw_re, tw_im)
    packs = spectrum_of(pair.astype(BF), fwd[...], line[...], tw_re, tw_im)
    backs_re, backs_im = [], []
    for spec, pack in zip(specs, packs):
        l_re, l_im = spec[:, :128], spec[:, 128:]
        p_re, p_im = pack[:, :128], pack[:, 128:]
        both = jnp.concatenate([l_re * p_re + l_im * p_im, l_im * p_re - l_re * p_im], axis=1)
        back = jnp.dot(both.astype(BF), line_back[...], preferred_element_type=F32)
        b_re, b_im = back[:, :128], back[:, 128:]
        backs_re.append(b_re * tw_re - b_im * tw_im)
        backs_im.append(b_re * tw_im + b_im * tw_re)
    stacked = jnp.concatenate(
        [jnp.concatenate(backs_re, axis=1), jnp.concatenate(backs_im, axis=1)], axis=0
    ).astype(BF)
    out = jnp.dot(inv[...], stacked, preferred_element_type=F32) * factor
    return out[:128].astype(BF).astype(F32), out[128:].astype(BF).astype(F32)


def local_kernel(factor, x_ref, fwd, inv, line, line_back, turn, o_ref, wide, narrow):
    wide[...] = x_ref[...].astype(F32)
    refs = (fwd, inv, line, line_back, turn)

    def pull(field, c):
        return jnp.concatenate(
            [wide[pl.ds(field * CH + c + h, DEV, FIELDS_IN * CH), :] for h in range(2)], axis=1
        )

    def push(field, c, data):
        for h in range(2):
            narrow[pl.ds(field * CH + c + h, DEV, FIELDS_OUT * CH), :] = data[
                :, h * 128 : h * 128 + 128
            ]

    def step(i, carry):
        c = 2 * i
        gate, conv = pull(GATE_ONE, c), pull(CONV_ONE, c)
        first_out = round_mul(gate, conv)
        grad_first, filter_two_grad = correlations(
            pull(GRAD_CONV_TWO, c),
            jnp.concatenate([pull(FILTER_TWO, c), first_out], axis=0),
            refs,
            factor,
        )
        push(1, c, round_mul(grad_first, conv))
        push(3, c, filter_two_grad)
        grad_value, filter_one_grad = correlations(
            round_mul(grad_first, gate),
            jnp.concatenate([pull(FILTER_ONE, c), pull(VALUE, c)], axis=0),
            refs,
            factor,
        )
        push(0, c, grad_value)
        push(2, c, filter_one_grad)
        return carry

    lax.fori_loop(0, CH // 2, step, 0)
    o_ref[...] = narrow[...].astype(BF)


def local_part(arrived, factor):
    tables = [jnp.asarray(t) for t in dft_tables()]
    flat = arrived.reshape(DEV * FIELDS_IN * CH, LANES)
    vmem = pl.BlockSpec(memory_space=pltpu.VMEM)
    out = pl.pallas_call(
        functools.partial(local_kernel, factor),
        out_shape=jax.ShapeDtypeStruct((DEV * FIELDS_OUT * CH, LANES), BF),
        in_specs=[vmem] * 6,
        out_specs=vmem,
        scratch_shapes=[
            pltpu.VMEM((DEV * FIELDS_IN * CH, LANES), F32),
            pltpu.VMEM((DEV * FIELDS_OUT * CH, LANES), F32),
        ],
        compiler_params=pltpu.CompilerParams(vmem_limit_bytes=56 << 20),
        name="local_part",
    )(flat, *tables)
    return out.reshape(DEV, FIELDS_OUT * CH, LANES)


def product(left, right):
    return (left.astype(F32) * right.astype(F32)).astype(BF)


def exchange(pieces):
    return lax.all_to_all(pieces, AXES, split_axis=0, concat_axis=0, tiled=True)


def shards(block_in, out_cot, w_in, w_out, conv_one, conv_two, filter_one, filter_two):
    rows, width = block_in.shape
    seq_len = rows * DEV
    scale = seq_len ** (-0.5)
    factor = scale / (2.0 * seq_len)
    contract_last = (((1,), (1,)), ((), ()))
    contract_first = (((0,), (0,)), ((), ()))
    proj = jnp.dot(block_in, w_in, preferred_element_type=F32).astype(BF)
    value, gate_one, gate_two = (proj[:, i * width : (i + 1) * width] for i in range(3))
    second_out = product(gate_two, conv_two)
    grad_second = lax.dot_general(
        out_cot, w_out, contract_last, preferred_element_type=F32
    ).astype(BF)
    grad_conv_two = product(grad_second, gate_two)
    grad_gate_two = product(grad_second, conv_two)
    fields = jnp.stack([value, gate_one, conv_one, filter_one, filter_two, grad_conv_two])
    fields = fields.reshape(FIELDS_IN, rows, DEV, CH).transpose(2, 0, 3, 1)
    arrived = exchange(fields.reshape(DEV, FIELDS_IN * CH, rows))
    back = exchange(local_part(arrived, factor)).reshape(DEV, FIELDS_OUT, CH, rows)
    back = back.transpose(1, 3, 0, 2).reshape(FIELDS_OUT, rows, width)
    grad_value, grad_gate_one, filter_one_grad, filter_two_grad = back
    grad_proj = jnp.concatenate([grad_value, grad_gate_one, grad_gate_two], axis=1)
    in_grad = lax.dot_general(
        grad_proj, w_in, contract_last, preferred_element_type=F32
    ).astype(BF)
    in_part = lax.dot_general(block_in, grad_proj, contract_first, preferred_element_type=F32)
    out_part = lax.dot_general(second_out, out_cot, contract_first, preferred_element_type=F32)
    parts = jnp.concatenate([in_part, out_part], axis=1).astype(BF)
    parts = exchange(parts.reshape(DEV, width // DEV, 4 * width))
    summed = jnp.sum(parts.astype(F32), axis=0) * scale
    return (
        in_grad,
        summed[:, : 3 * width],
        summed[:, 3 * width :],
        filter_one_grad,
        filter_two_grad,
    )


def solution(mesh):
    rows = P(AXES, None)
    return jax.shard_map(
        shards,
        mesh=mesh,
        in_specs=(rows, rows, P(), P(), rows, rows, rows, rows),
        out_specs=(rows,) * 5,
        check_vma=False,
    )
```

```python
import functools

import jax
import jax.numpy as jnp
import numpy as np
from jax import lax
from jax.experimental import pallas as pl
from jax.experimental.pallas import tpu as pltpu
from jax.sharding import PartitionSpec as P

AXES = ("major", "minor")
DEV = 128
CH = 8
LANES = 128
BF = jnp.bfloat16
F32 = jnp.float32
CONV_ONE, FILTER_TWO, GATE_ONE, GRAD_CONV_TWO, FILTER_ONE, VALUE = range(6)
GRAD_GATE_ONE, FILTER_TWO_GRAD, GRAD_VALUE, FILTER_ONE_GRAD = range(4)
FIELDS_IN = 6
FIELDS_OUT = 4
WAVE = 2 * CH
MESH = pl.DeviceIdType.MESH


def dft_tables():
    k1 = np.arange(256)[:, None]
    n1 = np.arange(128)[None, :]
    a = 2.0 * np.pi * ((k1 * n1) % 256) / 256
    c, s = np.cos(a), np.sin(a)
    n2 = np.arange(128)
    b = 2.0 * np.pi * ((n2[:, None] * n2[None, :]) % 128) / 128
    cb, sb = np.cos(b), np.sin(b)
    t = 2.0 * np.pi * (k1 * n2[None, :]) / 32768
    return (
        np.block([[c, -s], [-s, -c]]).astype(BF),
        np.block([[c.T, -s.T], [s.T, c.T]]).astype(BF),
        np.block([[cb, -sb], [sb, cb]]).astype(BF),
        np.block([[cb, sb], [-sb, cb]]).astype(BF),
        np.stack([np.cos(t), np.sin(t)]).astype(np.float32),
    )


def round_mul(a, b):
    return (a * b).astype(BF).astype(F32)


def spectrum_of(data, table, line, tw_re, tw_im):
    grid = jnp.dot(table, data, preferred_element_type=F32)
    out = []
    for h in range(2):
        re = grid[:256, h * 128 : h * 128 + 128]
        im = grid[256:, h * 128 : h * 128 + 128]
        turned = jnp.concatenate([re * tw_re + im * tw_im, im * tw_re - re * tw_im], axis=1)
        out.append(jnp.dot(turned.astype(BF), line, preferred_element_type=F32))
    return out


def correlations(left, pair, refs, factor):
    fwd, inv, line, line_back, turn = refs
    tw_re, tw_im = turn[0], turn[1]
    specs = spectrum_of(left.astype(BF), fwd[:, :128], line[...], tw_re, tw_im)
    packs = spectrum_of(pair.astype(BF), fwd[...], line[...], tw_re, tw_im)
    backs_re, backs_im = [], []
    for spec, pack in zip(specs, packs):
        l_re, l_im = spec[:, :128], spec[:, 128:]
        p_re, p_im = pack[:, :128], pack[:, 128:]
        both = jnp.concatenate([l_re * p_re + l_im * p_im, l_im * p_re - l_re * p_im], axis=1)
        back = jnp.dot(both.astype(BF), line_back[...], preferred_element_type=F32)
        b_re, b_im = back[:, :128], back[:, 128:]
        backs_re.append(b_re * tw_re - b_im * tw_im)
        backs_im.append(b_re * tw_im + b_im * tw_re)
    stacked = jnp.concatenate(
        [jnp.concatenate(backs_re, axis=1), jnp.concatenate(backs_im, axis=1)], axis=0
    ).astype(BF)
    out = jnp.dot(inv[...], stacked, preferred_element_type=F32) * factor
    return out[:128].astype(BF).astype(F32), out[128:].astype(BF).astype(F32)


def peer_of(step):
    major, minor = lax.axis_index("major"), lax.axis_index("minor")
    x = (minor // 2) % 2 * 2 + major // 4
    x = (x + (step // 2) % 4) % 4
    y = (major % 4 + (step // 8) % 4) % 4
    z = (minor // 4 + step // 32) % 4
    core = (minor + step) % 2
    return (x % 2 * 4 + y, z * 4 + x // 2 * 2 + core)


def my_index():
    return lax.axis_index("major") * 16 + lax.axis_index("minor")


def greet_all():
    barrier = pltpu.get_barrier_semaphore()

    def signal(step, carry):
        pl.semaphore_signal(barrier, inc=1, device_id=peer_of(step), device_id_type=MESH)
        return carry

    lax.fori_loop(1, DEV, signal, 0)
    pl.semaphore_wait(barrier, DEV - 1)


def send_wave(src, dst, send_sem, recv_sem, own_sem):
    me = my_index()
    pltpu.make_async_copy(src.at[me], dst.at[me], own_sem).start()

    def send(step, carry):
        major, minor = peer_of(step)
        pltpu.make_async_remote_copy(
            src_ref=src.at[major * 16 + minor],
            dst_ref=dst.at[me],
            send_sem=send_sem,
            recv_sem=recv_sem,
            device_id=(major, minor),
            device_id_type=MESH,
        ).start()
        return carry

    lax.fori_loop(1, DEV, send, 0)


def wait_wave(src, dst, sem, own_sem=None):
    if own_sem is not None:
        me = my_index()
        pltpu.make_async_copy(src.at[me], dst.at[me], own_sem).wait()
    most = pl.ds(0, DEV - 1)
    pltpu.make_async_copy(src.at[most], dst.at[most], sem).wait()


def local_kernel(
    factor, x0, x1, x2, fwd, inv, line, line_back, turn, o0, o1,
    r0, r1, r2, b0, b1, wide, narrow, send_sems, recv_sems, own_sems,
):
    refs = (fwd, inv, line, line_back, turn)
    greet_all()
    waves = ((x0, r0), (x1, r1), (x2, r2))
    for k, (src, dst) in enumerate(waves):
        send_wave(src, dst, send_sems.at[k], recv_sems.at[k], own_sems.at[k])

    def receive(k):
        src, dst = waves[k]
        wait_wave(src, dst, recv_sems.at[k], own_sems.at[k])
        wide[k] = dst[...].astype(F32).reshape(DEV * WAVE, LANES)

    def pull(field, c):
        start = field % 2 * CH + c
        return jnp.concatenate(
            [wide[field // 2, pl.ds(start + h, DEV, WAVE), :] for h in range(2)], axis=1
        )

    def push(field, c, data):
        for h in range(2):
            narrow[field // 2, pl.ds(field % 2 * CH + c + h, DEV, WAVE), :] = data[
                :, h * 128 : h * 128 + 128
            ]

    def first(i, carry):
        c = 2 * i
        gate, conv = pull(GATE_ONE, c), pull(CONV_ONE, c)
        first_out = round_mul(gate, conv)
        grad_first, filter_two_grad = correlations(
            pull(GRAD_CONV_TWO, c),
            jnp.concatenate([pull(FILTER_TWO, c), first_out], axis=0),
            refs,
            factor,
        )
        push(GRAD_GATE_ONE, c, round_mul(grad_first, conv))
        push(FILTER_TWO_GRAD, c, filter_two_grad)
        for h in range(2):
            wide[1, pl.ds(GATE_ONE % 2 * CH + c + h, DEV, WAVE), :] = round_mul(grad_first, gate)[
                :, h * 128 : h * 128 + 128
            ]
        return carry

    def second(i, carry):
        c = 2 * i
        grad_value, filter_one_grad = correlations(
            pull(GATE_ONE, c),
            jnp.concatenate([pull(FILTER_ONE, c), pull(VALUE, c)], axis=0),
            refs,
            factor,
        )
        push(GRAD_VALUE, c, grad_value)
        push(FILTER_ONE_GRAD, c, filter_one_grad)
        return carry

    receive(0)
    receive(1)
    lax.fori_loop(0, CH // 2, first, 0)
    b0[...] = narrow[0].astype(BF).reshape(DEV, WAVE, LANES)
    send_wave(b0, o0, send_sems.at[3], recv_sems.at[3], own_sems.at[3])
    receive(2)
    lax.fori_loop(0, CH // 2, second, 0)
    b1[...] = narrow[1].astype(BF).reshape(DEV, WAVE, LANES)
    send_wave(b1, o1, send_sems.at[4], recv_sems.at[4], own_sems.at[4])
    for k, (src, dst) in enumerate(waves):
        wait_wave(src, dst, send_sems.at[k])
    for k, (src, dst) in enumerate(((b0, o0), (b1, o1)), 3):
        wait_wave(src, dst, recv_sems.at[k], own_sems.at[k])
        wait_wave(src, dst, send_sems.at[k])


def local_part(fields, factor):
    tables = [jnp.asarray(t) for t in dft_tables()]
    vmem = pl.BlockSpec(memory_space=pltpu.VMEM)
    piece = (DEV, WAVE, LANES)
    return pl.pallas_call(
        functools.partial(local_kernel, factor),
        out_shape=(jax.ShapeDtypeStruct(piece, BF),) * 2,
        in_specs=[vmem] * 8,
        out_specs=(vmem,) * 2,
        scratch_shapes=[pltpu.VMEM(piece, BF)] * 5
        + [
            pltpu.VMEM((3, DEV * WAVE, LANES), F32),
            pltpu.VMEM((2, DEV * WAVE, LANES), F32),
            pltpu.SemaphoreType.DMA((5,)),
            pltpu.SemaphoreType.DMA((5,)),
            pltpu.SemaphoreType.DMA((5,)),
        ],
        compiler_params=pltpu.CompilerParams(
            vmem_limit_bytes=56 << 20, collective_id=0, has_side_effects=True
        ),
        name="local_part",
    )(*fields, *tables)


def product(left, right):
    return (left.astype(F32) * right.astype(F32)).astype(BF)


def exchange(pieces):
    return lax.all_to_all(pieces, AXES, split_axis=0, concat_axis=0, tiled=True)


def shards(block_in, out_cot, w_in, w_out, conv_one, conv_two, filter_one, filter_two):
    rows, width = block_in.shape
    seq_len = rows * DEV
    scale = seq_len ** (-0.5)
    factor = scale / (2.0 * seq_len)
    contract_last = (((1,), (1,)), ((), ()))
    contract_first = (((0,), (0,)), ((), ()))
    proj = jnp.dot(block_in, w_in, preferred_element_type=F32).astype(BF)
    value, gate_one, gate_two = (proj[:, i * width : (i + 1) * width] for i in range(3))
    second_out = product(gate_two, conv_two)
    grad_second = lax.dot_general(
        out_cot, w_out, contract_last, preferred_element_type=F32
    ).astype(BF)
    grad_conv_two = product(grad_second, gate_two)
    grad_gate_two = product(grad_second, conv_two)
    def pieces(one, two):
        pair = jnp.stack([one, two]).reshape(2, rows, DEV, CH).transpose(2, 0, 3, 1)
        return pair.reshape(DEV, WAVE, rows)

    def steps(pair):
        pair = pair.reshape(DEV, 2, CH, rows).transpose(1, 3, 0, 2)
        return pair.reshape(2, rows, width)

    back = local_part(
        (pieces(conv_one, filter_two), pieces(gate_one, grad_conv_two), pieces(filter_one, value)),
        factor,
    )
    grad_gate_one, filter_two_grad = steps(back[0])
    grad_value, filter_one_grad = steps(back[1])
    grad_proj = jnp.concatenate([grad_value, grad_gate_one, grad_gate_two], axis=1)
    in_grad = lax.dot_general(
        grad_proj, w_in, contract_last, preferred_element_type=F32
    ).astype(BF)
    in_part = lax.dot_general(block_in, grad_proj, contract_first, preferred_element_type=F32)
    out_part = lax.dot_general(second_out, out_cot, contract_first, preferred_element_type=F32)
    parts = jnp.concatenate([in_part, out_part], axis=1).astype(BF)
    parts = exchange(parts.reshape(DEV, width // DEV, 4 * width))
    summed = jnp.sum(parts.astype(F32), axis=0) * scale
    return (
        in_grad,
        summed[:, : 3 * width],
        summed[:, 3 * width :],
        filter_one_grad,
        filter_two_grad,
    )


def solution(mesh):
    rows = P(AXES, None)
    return jax.shard_map(
        shards,
        mesh=mesh,
        in_specs=(rows, rows, P(), P(), rows, rows, rows, rows),
        out_specs=(rows,) * 5,
        check_vma=False,
    )
```

```python
import functools

import jax
import jax.numpy as jnp
import numpy as np
from jax import lax
from jax.experimental import pallas as pl
from jax.experimental.pallas import tpu as pltpu
from jax.sharding import PartitionSpec as P

AXES = ("major", "minor")
DEV = 128
CH = 8
LANES = 128
BF = jnp.bfloat16
F32 = jnp.float32
CONV_ONE, FILTER_TWO, GATE_ONE, GRAD_CONV_TWO, FILTER_ONE, VALUE = range(6)
GRAD_GATE_ONE, FILTER_TWO_GRAD, GRAD_VALUE, FILTER_ONE_GRAD = range(4)
FIELDS_IN = 6
FIELDS_OUT = 4
WAVE = 2 * CH
MESH = pl.DeviceIdType.MESH


def dft_tables():
    k1 = np.arange(256)[:, None]
    n1 = np.arange(128)[None, :]
    a = 2.0 * np.pi * ((k1 * n1) % 256) / 256
    c, s = np.cos(a), np.sin(a)
    n2 = np.arange(128)
    b = 2.0 * np.pi * ((n2[:, None] * n2[None, :]) % 128) / 128
    cb, sb = np.cos(b), np.sin(b)
    t = 2.0 * np.pi * (k1 * n2[None, :]) / 32768
    return (
        np.block([[c, -s], [-s, -c]]).astype(BF),
        np.block([[c.T, -s.T], [s.T, c.T]]).astype(BF),
        np.block([[cb, -sb], [sb, cb]]).astype(BF),
        np.block([[cb, sb], [-sb, cb]]).astype(BF),
        np.stack([np.cos(t), np.sin(t)]).astype(np.float32),
    )


def round_mul(a, b):
    return (a * b).astype(BF).astype(F32)


def spectrum_of(data, table, line, tw_re, tw_im):
    grid = jnp.dot(table, data, preferred_element_type=F32)
    out = []
    for h in range(2):
        re = grid[:256, h * 128 : h * 128 + 128]
        im = grid[256:, h * 128 : h * 128 + 128]
        turned = jnp.concatenate([re * tw_re + im * tw_im, im * tw_re - re * tw_im], axis=1)
        out.append(jnp.dot(turned.astype(BF), line, preferred_element_type=F32))
    return out


def correlations(left, pair, refs, factor):
    fwd, inv, line, line_back, turn = refs
    tw_re, tw_im = turn[0], turn[1]
    specs = spectrum_of(left.astype(BF), fwd[:, :128], line[...], tw_re, tw_im)
    packs = spectrum_of(pair.astype(BF), fwd[...], line[...], tw_re, tw_im)
    backs_re, backs_im = [], []
    for spec, pack in zip(specs, packs):
        l_re, l_im = spec[:, :128], spec[:, 128:]
        p_re, p_im = pack[:, :128], pack[:, 128:]
        both = jnp.concatenate([l_re * p_re + l_im * p_im, l_im * p_re - l_re * p_im], axis=1)
        back = jnp.dot(both.astype(BF), line_back[...], preferred_element_type=F32)
        b_re, b_im = back[:, :128], back[:, 128:]
        backs_re.append(b_re * tw_re - b_im * tw_im)
        backs_im.append(b_re * tw_im + b_im * tw_re)
    stacked = jnp.concatenate(
        [jnp.concatenate(backs_re, axis=1), jnp.concatenate(backs_im, axis=1)], axis=0
    ).astype(BF)
    out = jnp.dot(inv[...], stacked, preferred_element_type=F32) * factor
    return out[:128].astype(BF).astype(F32), out[128:].astype(BF).astype(F32)


def peer_of(step):
    major, minor = lax.axis_index("major"), lax.axis_index("minor")
    x = (minor // 2) % 2 * 2 + major // 4
    x = (x + (step // 2) % 4) % 4
    y = (major % 4 + (step // 8) % 4) % 4
    z = (minor // 4 + step // 32) % 4
    core = (minor + step) % 2
    return (x % 2 * 4 + y, z * 4 + x // 2 * 2 + core)


def my_index():
    return lax.axis_index("major") * 16 + lax.axis_index("minor")


def greet_all():
    barrier = pltpu.get_barrier_semaphore()

    def signal(step, carry):
        pl.semaphore_signal(barrier, inc=1, device_id=peer_of(step), device_id_type=MESH)
        return carry

    lax.fori_loop(1, DEV, signal, 0)
    pl.semaphore_wait(barrier, DEV - 1)


def send_wave(src, dst, send_sem, recv_sem, own_sem):
    me = my_index()
    pltpu.make_async_copy(src.at[me], dst.at[me], own_sem).start()

    def send(step, carry):
        major, minor = peer_of(step)
        pltpu.make_async_remote_copy(
            src_ref=src.at[major * 16 + minor],
            dst_ref=dst.at[me],
            send_sem=send_sem,
            recv_sem=recv_sem,
            device_id=(major, minor),
            device_id_type=MESH,
        ).start()
        return carry

    lax.fori_loop(1, DEV, send, 0)


def wait_wave(src, dst, sem, own_sem=None):
    if own_sem is not None:
        me = my_index()
        pltpu.make_async_copy(src.at[me], dst.at[me], own_sem).wait()
    most = pl.ds(0, DEV - 1)
    pltpu.make_async_copy(src.at[most], dst.at[most], sem).wait()


def local_kernel(
    factor, x0, x1, x2, fwd, inv, line, line_back, turn, o0, o1,
    r0, r1, r2, b0, b1, wide, narrow, send_sems, recv_sems, own_sems,
):
    refs = (fwd, inv, line, line_back, turn)
    greet_all()
    waves = ((x0, r0), (x1, r1), (x2, r2))
    for k, (src, dst) in enumerate(waves):
        send_wave(src, dst, send_sems.at[k], recv_sems.at[k], own_sems.at[k])

    def receive(k):
        src, dst = waves[k]
        wait_wave(src, dst, recv_sems.at[k], own_sems.at[k])
        wide[k] = dst[...].astype(F32).reshape(DEV * WAVE, LANES)

    def pull(field, c):
        start = field % 2 * CH + c
        return jnp.concatenate(
            [wide[field // 2, pl.ds(start + h, DEV, WAVE), :] for h in range(2)], axis=1
        )

    def push(field, c, data):
        for h in range(2):
            narrow[field // 2, pl.ds(field % 2 * CH + c + h, DEV, WAVE), :] = data[
                :, h * 128 : h * 128 + 128
            ]

    def first(i, carry):
        c = 2 * i
        gate, conv = pull(GATE_ONE, c), pull(CONV_ONE, c)
        first_out = round_mul(gate, conv)
        grad_first, filter_two_grad = correlations(
            pull(GRAD_CONV_TWO, c),
            jnp.concatenate([pull(FILTER_TWO, c), first_out], axis=0),
            refs,
            factor,
        )
        push(GRAD_GATE_ONE, c, round_mul(grad_first, conv))
        push(FILTER_TWO_GRAD, c, filter_two_grad)
        for h in range(2):
            wide[1, pl.ds(GATE_ONE % 2 * CH + c + h, DEV, WAVE), :] = round_mul(grad_first, gate)[
                :, h * 128 : h * 128 + 128
            ]
        return carry

    def second(i, carry):
        c = 2 * i
        grad_value, filter_one_grad = correlations(
            pull(GATE_ONE, c),
            jnp.concatenate([pull(FILTER_ONE, c), pull(VALUE, c)], axis=0),
            refs,
            factor,
        )
        push(GRAD_VALUE, c, grad_value)
        push(FILTER_ONE_GRAD, c, filter_one_grad)
        return carry

    receive(0)
    receive(1)
    lax.fori_loop(0, CH // 2, first, 0)
    b0[...] = narrow[0].astype(BF).reshape(DEV, WAVE, LANES)
    send_wave(b0, o0, send_sems.at[3], recv_sems.at[3], own_sems.at[3])
    receive(2)
    lax.fori_loop(0, CH // 2, second, 0)
    b1[...] = narrow[1].astype(BF).reshape(DEV, WAVE, LANES)
    send_wave(b1, o1, send_sems.at[4], recv_sems.at[4], own_sems.at[4])
    for k, (src, dst) in enumerate(waves):
        wait_wave(src, dst, send_sems.at[k])
    for k, (src, dst) in enumerate(((b0, o0), (b1, o1)), 3):
        wait_wave(src, dst, recv_sems.at[k], own_sems.at[k])
        wait_wave(src, dst, send_sems.at[k])


def local_part(fields, factor):
    tables = [jnp.asarray(t) for t in dft_tables()]
    vmem = pl.BlockSpec(memory_space=pltpu.VMEM)
    piece = (DEV, WAVE, LANES)
    return pl.pallas_call(
        functools.partial(local_kernel, factor),
        out_shape=(jax.ShapeDtypeStruct(piece, BF),) * 2,
        in_specs=[vmem] * 8,
        out_specs=(vmem,) * 2,
        scratch_shapes=[pltpu.VMEM(piece, BF)] * 5
        + [
            pltpu.VMEM((3, DEV * WAVE, LANES), F32),
            pltpu.VMEM((2, DEV * WAVE, LANES), F32),
            pltpu.SemaphoreType.DMA((5,)),
            pltpu.SemaphoreType.DMA((5,)),
            pltpu.SemaphoreType.DMA((5,)),
        ],
        compiler_params=pltpu.CompilerParams(
            vmem_limit_bytes=56 << 20, collective_id=0, has_side_effects=True
        ),
        name="local_part",
    )(*fields, *tables)


HALF = 512
SHARES = {
    (0, 0): [(0, 2, 0, 256), (1, 3, 0, 128)],
    (0, 1): [(0, 2, 256, 128), (1, 3, 128, 256)],
    (0, 2): [(0, 2, 384, 128), (1, 3, 384, 128)],
    (1, 0): [(0, 0, 0, 128), (0, 1, 0, 128)],
    (1, 1): [(0, 0, 128, 128), (0, 1, 128, 256)],
    (1, 2): [(0, 0, 256, 256), (0, 1, 384, 128)],
}
ORDERS = (("y", "z", "x"), ("z", "x", "y"), ("x", "y", "z"))
UNITS = [(w, g) for w in range(2) for g in range(3)]


def width_of(unit):
    return sum(share[3] for share in SHARES[unit])


def coordinates():
    major, minor = lax.axis_index("major"), lax.axis_index("minor")
    x = (minor // 2) % 2 * 2 + major // 4
    return {"x": x, "y": major % 4, "z": minor // 4, "core": minor % 2}


def device_at(at):
    return (at["x"] % 2 * 4 + at["y"], at["z"] * 4 + at["x"] // 2 * 2 + at["core"])


def moved(at, dim, step):
    return dict(at, **{dim: (at[dim] + step) % (2 if dim == "core" else 4)})


def rows_at(phase, group, value):
    every = slice(None)
    if group == 0:
        return [(every, value), (every, value), (value % 2, value // 2)][phase]
    if group == 1:
        return [(every, every, value), (value % 2, every, value // 2), (value,)][phase]
    return [(value % 2, every, every, value // 2), (value,), (value,)][phase]


SUMMED = (
    ((2, 4, 2), (2, 2), ()),
    ((2, 4, 2), (4,), ()),
    ((4, 4), (4,), ()),
)


def weight_kernel(
    scale, a1, a2, b0, b1, b2, b3, in_ref, out_ref,
    left, left_peer, right_peer, own, got, sums, parts, last,
    pair_sems, send_sems, recv_sems, final_sems,
):
    at = coordinates()
    core = at["core"]
    partner = device_at(moved(at, "core", 1))
    barrier = pltpu.get_barrier_semaphore()
    peers = [partner] + [device_at(moved(at, d, k)) for d in "xyz" for k in (1, 2, 3)]
    for peer in peers:
        pl.semaphore_signal(barrier, inc=1, device_id=peer, device_id_type=MESH)
    pl.semaphore_wait(barrier, len(peers))

    theirs = pl.ds(pl.multiple_of((1 - core) * HALF, HALF), HALF)
    mine = pl.ds(pl.multiple_of(core * HALF, HALF), HALF)
    copies = []

    def remote(src, dst, send_sem, recv_sem, device):
        copy = pltpu.make_async_remote_copy(
            src_ref=src, dst_ref=dst, send_sem=send_sem, recv_sem=recv_sem,
            device_id=device, device_id_type=MESH,
        )
        copy.start()
        copies.append(copy)
        return copy

    pair = [
        remote(src, dst, pair_sems.at[0, k], pair_sems.at[1, k], partner)
        for k, (src, dst) in enumerate(
            [(a1, left_peer.at[0]), (b2.at[:, theirs], right_peer.at[2])]
            + [(a2, left_peer.at[1]), (b3.at[:, theirs], right_peer.at[3])]
            + [(b0.at[:, theirs], right_peer.at[0]), (b1.at[:, theirs], right_peer.at[1])]
        )
    ]
    shape = (2, 4, 4, 2, 16, 128)
    for k, ref in enumerate((a1, a2)):
        left[k, :, :, :, :, :, :128] = ref[...].T.reshape(shape)
    for k in range(2):
        pair[2 * k].wait_recv()
        left[k, :, :, :, :, :, 128:] = left_peer[k].T.reshape(shape)

    rights = (b0, b1, b2, b3)
    arrived = {2: 1, 3: 3, 0: 4, 1: 5}
    waited = set()
    for u, unit in enumerate(UNITS):
        group = unit[1]
        dim = ORDERS[group][0]
        for step in (2, 1, 3, 0):
            index = rows_at(0, group, (at[dim] + step) % 4)
            col = 0
            for which, block, first, width in SHARES[unit]:
                if block not in waited:
                    waited.add(block)
                    pair[arrived[block]].wait_recv()
                rows = left[(which,) + index].reshape(256, 256)
                cols = pl.ds(pl.multiple_of(core * HALF + first, 128), width)
                right = jnp.concatenate(
                    [rights[block][:, cols], right_peer[block, :, first : first + width]], axis=0
                )
                own[u][step, ..., col : col + width] = (
                    jnp.dot(rows, right, preferred_element_type=F32)
                    .astype(BF)
                    .reshape(SUMMED[group][0] + (16, width))
                )
                col += width
            if step:
                remote(
                    own[u].at[step], got[u][0].at[step - 1], send_sems.at[u, 0, step - 1],
                    recv_sems.at[u, 0, step - 1], device_at(moved(at, dim, step)),
                )
    for phase in range(3):
        for u, unit in enumerate(UNITS):
            group = unit[1]
            base = own[u].at[0] if phase == 0 else sums[u][phase - 1]
            index = () if phase == 0 else rows_at(phase, group, at[ORDERS[group][phase]])
            total = base[index + (Ellipsis,)].astype(F32)
            for k in range(3):
                pltpu.make_async_copy(
                    got[u][phase].at[k], got[u][phase].at[k], recv_sems.at[u, phase, k]
                ).wait()
                total = total + got[u][phase][k].astype(F32)
            if phase == 2:
                parts[u][...] = (total * scale).reshape(2, 8, width_of(unit))
                remote(
                    parts[u].at[1 - core], last[u], final_sems.at[0, u], final_sems.at[1, u], partner
                )
                continue
            sums[u][phase][...] = total.astype(BF)
            dim = ORDERS[group][phase + 1]
            for step in (2, 1, 3):
                index = rows_at(phase + 1, group, (at[dim] + step) % 4)
                remote(
                    sums[u][phase].at[index], got[u][phase + 1].at[step - 1],
                    send_sems.at[u, phase + 1, step - 1], recv_sems.at[u, phase + 1, step - 1],
                    device_at(moved(at, dim, step)),
                )
    for u, unit in enumerate(UNITS):
        pltpu.make_async_copy(last[u], last[u], final_sems.at[1, u]).wait()
        col = 0
        for which, block, first, width in SHARES[unit]:
            target, start = (out_ref, 0) if which else (in_ref, block * 2 * HALF)
            for part, half in ((parts[u].at[core], core), (last[u], 1 - core)):
                cols = pl.ds(pl.multiple_of(start + half * HALF + first, 128), width)
                target[:, cols] = part[:, col : col + width]
            col += width
    for copy in copies:
        copy.wait_send()


def weight_grads(block_in, second_out, blocks, scale):
    vmem = pl.BlockSpec(memory_space=pltpu.VMEM)
    width = block_in.shape[1]
    own, got, sums, parts, last = [], [], [], [], []
    for unit in UNITS:
        w = width_of(unit)
        shapes = [shape + (16, w) for shape in SUMMED[unit[1]]]
        own.append(pltpu.VMEM((4,) + shapes[0], BF))
        got.append([pltpu.VMEM((3,) + shape, BF) for shape in shapes])
        sums.append([pltpu.VMEM(shape, BF) for shape in shapes[:2]])
        parts.append(pltpu.VMEM((2, 8, w), F32))
        last.append(pltpu.VMEM((8, w), F32))
    return pl.pallas_call(
        functools.partial(weight_kernel, scale),
        out_shape=(
            jax.ShapeDtypeStruct((width // DEV, 3 * width), F32),
            jax.ShapeDtypeStruct((width // DEV, width), F32),
        ),
        in_specs=[vmem] * 6,
        out_specs=(vmem,) * 2,
        scratch_shapes=[
            pltpu.VMEM((2, 2, 4, 4, 2, 16, 256), BF),
            pltpu.VMEM((2, 128, width), BF),
            pltpu.VMEM((4, 128, HALF), BF),
            own, got, sums, parts, last,
            pltpu.SemaphoreType.DMA((2, 6)),
            pltpu.SemaphoreType.DMA((6, 3, 3)),
            pltpu.SemaphoreType.DMA((6, 3, 3)),
            pltpu.SemaphoreType.DMA((2, 6)),
        ],
        compiler_params=pltpu.CompilerParams(
            vmem_limit_bytes=56 << 20, collective_id=1, has_side_effects=True
        ),
        name="weight_grads",
    )(block_in, second_out, *blocks)


def product(left, right):
    return (left.astype(F32) * right.astype(F32)).astype(BF)


def shards(block_in, out_cot, w_in, w_out, conv_one, conv_two, filter_one, filter_two):
    rows, width = block_in.shape
    seq_len = rows * DEV
    scale = seq_len ** (-0.5)
    factor = scale / (2.0 * seq_len)
    contract_last = (((1,), (1,)), ((), ()))
    proj = jnp.dot(block_in, w_in, preferred_element_type=F32).astype(BF)
    value, gate_one, gate_two = (proj[:, i * width : (i + 1) * width] for i in range(3))
    second_out = product(gate_two, conv_two)
    grad_second = lax.dot_general(
        out_cot, w_out, contract_last, preferred_element_type=F32
    ).astype(BF)
    grad_conv_two = product(grad_second, gate_two)
    grad_gate_two = product(grad_second, conv_two)
    def pieces(one, two):
        pair = jnp.stack([one, two]).reshape(2, rows, DEV, CH).transpose(2, 0, 3, 1)
        return pair.reshape(DEV, WAVE, rows)

    def steps(pair):
        pair = pair.reshape(DEV, 2, CH, rows).transpose(1, 3, 0, 2)
        return pair.reshape(2, rows, width)

    back = local_part(
        (pieces(conv_one, filter_two), pieces(gate_one, grad_conv_two), pieces(filter_one, value)),
        factor,
    )
    grad_gate_one, filter_two_grad = steps(back[0])
    grad_value, filter_one_grad = steps(back[1])
    grad_proj = jnp.concatenate([grad_value, grad_gate_one, grad_gate_two], axis=1)
    in_grad = lax.dot_general(
        grad_proj, w_in, contract_last, preferred_element_type=F32
    ).astype(BF)
    in_part, out_part = weight_grads(
        block_in, second_out, (grad_value, grad_gate_one, grad_gate_two, out_cot), scale
    )
    return (in_grad, in_part, out_part, filter_one_grad, filter_two_grad)


def solution(mesh):
    rows = P(AXES, None)
    return jax.shard_map(
        shards,
        mesh=mesh,
        in_specs=(rows, rows, P(), P(), rows, rows, rows, rows),
        out_specs=(rows,) * 5,
        check_vma=False,
    )
```

```python
import functools

import jax
import jax.numpy as jnp
import numpy as np
from jax import lax
from jax.experimental import pallas as pl
from jax.experimental.pallas import tpu as pltpu
from jax.sharding import PartitionSpec as P

AXES = ("major", "minor")
DEV = 128
CH = 8
LANES = 128
BF = jnp.bfloat16
F32 = jnp.float32
CONV_ONE, FILTER_TWO, GATE_ONE, GRAD_CONV_TWO, FILTER_ONE, VALUE = range(6)
GRAD_GATE_ONE, FILTER_TWO_GRAD, GRAD_VALUE, FILTER_ONE_GRAD = range(4)
FIELDS_IN = 6
FIELDS_OUT = 4
WAVE = 2 * CH
MESH = pl.DeviceIdType.MESH


def dft_tables():
    k1 = np.arange(256)[:, None]
    n1 = np.arange(128)[None, :]
    a = 2.0 * np.pi * ((k1 * n1) % 256) / 256
    c, s = np.cos(a), np.sin(a)
    n2 = np.arange(128)
    b = 2.0 * np.pi * ((n2[:, None] * n2[None, :]) % 128) / 128
    cb, sb = np.cos(b), np.sin(b)
    t = 2.0 * np.pi * (k1 * n2[None, :]) / 32768
    return (
        np.block([[c, -s], [-s, -c]]).astype(BF),
        np.block([[c.T, -s.T], [s.T, c.T]]).astype(BF),
        np.block([[cb, -sb], [sb, cb]]).astype(BF),
        np.block([[cb, sb], [-sb, cb]]).astype(BF),
        np.stack([np.cos(t), np.sin(t)]).astype(np.float32),
    )


def round_mul(a, b):
    return (a * b).astype(BF).astype(F32)


def spectrum_of(data, table, line, tw_re, tw_im):
    grid = jnp.dot(table, data, preferred_element_type=F32)
    out = []
    for h in range(2):
        re = grid[:256, h * 128 : h * 128 + 128]
        im = grid[256:, h * 128 : h * 128 + 128]
        turned = jnp.concatenate([re * tw_re + im * tw_im, im * tw_re - re * tw_im], axis=1)
        out.append(jnp.dot(turned.astype(BF), line, preferred_element_type=F32))
    return out


def correlations(left, pair, refs, factor):
    fwd, inv, line, line_back, turn = refs
    tw_re, tw_im = turn[0], turn[1]
    specs = spectrum_of(left.astype(BF), fwd[:, :128], line[...], tw_re, tw_im)
    packs = spectrum_of(pair.astype(BF), fwd[...], line[...], tw_re, tw_im)
    backs_re, backs_im = [], []
    for spec, pack in zip(specs, packs):
        l_re, l_im = spec[:, :128], spec[:, 128:]
        p_re, p_im = pack[:, :128], pack[:, 128:]
        both = jnp.concatenate([l_re * p_re + l_im * p_im, l_im * p_re - l_re * p_im], axis=1)
        back = jnp.dot(both.astype(BF), line_back[...], preferred_element_type=F32)
        b_re, b_im = back[:, :128], back[:, 128:]
        backs_re.append(b_re * tw_re - b_im * tw_im)
        backs_im.append(b_re * tw_im + b_im * tw_re)
    stacked = jnp.concatenate(
        [jnp.concatenate(backs_re, axis=1), jnp.concatenate(backs_im, axis=1)], axis=0
    ).astype(BF)
    out = jnp.dot(inv[...], stacked, preferred_element_type=F32) * factor
    return out[:128].astype(BF).astype(F32), out[128:].astype(BF).astype(F32)


def peer_of(step):
    step = step * 37 % DEV
    major, minor = lax.axis_index("major"), lax.axis_index("minor")
    x = (minor // 2) % 2 * 2 + major // 4
    x = (x + (step // 2) % 4) % 4
    y = (major % 4 + (step // 8) % 4) % 4
    z = (minor // 4 + step // 32) % 4
    core = (minor + step) % 2
    return (x % 2 * 4 + y, z * 4 + x // 2 * 2 + core)


def my_index():
    return lax.axis_index("major") * 16 + lax.axis_index("minor")


def send_wave(src, dst, send_sem, recv_sem, own_sem):
    me = my_index()
    pltpu.make_async_copy(src.at[me], dst.at[me], own_sem).start()

    def send(step, carry):
        major, minor = peer_of(step)
        pltpu.make_async_remote_copy(
            src_ref=src.at[major * 16 + minor],
            dst_ref=dst.at[me],
            send_sem=send_sem,
            recv_sem=recv_sem,
            device_id=(major, minor),
            device_id_type=MESH,
        ).start()
        return carry

    lax.fori_loop(1, DEV, send, 0)


def wait_wave(src, dst, sem, own_sem=None):
    if own_sem is not None:
        me = my_index()
        pltpu.make_async_copy(src.at[me], dst.at[me], own_sem).wait()
    most = pl.ds(0, DEV - 1)
    pltpu.make_async_copy(src.at[most], dst.at[most], sem).wait()


HALF = 512
SHARES = {
    (0, 0): [(0, 2, 0, 256), (1, 3, 0, 128)],
    (0, 1): [(0, 2, 256, 128), (1, 3, 128, 256)],
    (0, 2): [(0, 2, 384, 128), (1, 3, 384, 128)],
    (1, 0): [(0, 1, 0, 128)],
    (1, 1): [(0, 1, 128, 128)],
    (1, 2): [(0, 1, 256, 256)],
    (2, 0): [(0, 0, 0, 256)],
    (2, 1): [(0, 0, 256, 128)],
    (2, 2): [(0, 0, 384, 128)],
}
ORDERS = (("y", "z", "x"), ("z", "x", "y"), ("x", "y", "z"))
UNITS = [(w, g) for w in range(3) for g in range(3)]


def width_of(unit):
    return sum(share[3] for share in SHARES[unit])


def coordinates():
    major, minor = lax.axis_index("major"), lax.axis_index("minor")
    x = (minor // 2) % 2 * 2 + major // 4
    return {"x": x, "y": major % 4, "z": minor // 4, "core": minor % 2}


def device_at(at):
    return (at["x"] % 2 * 4 + at["y"], at["z"] * 4 + at["x"] // 2 * 2 + at["core"])


def moved(at, dim, step):
    return dict(at, **{dim: (at[dim] + step) % (2 if dim == "core" else 4)})


def rows_at(phase, group, value):
    every = slice(None)
    if group == 0:
        return [(every, value), (every, value), (value % 2, value // 2)][phase]
    if group == 1:
        return [(every, every, value), (value % 2, every, value // 2), (value,)][phase]
    return [(value % 2, every, every, value // 2), (value,), (value,)][phase]


SUMMED = (
    ((2, 4, 2), (2, 2), ()),
    ((2, 4, 2), (4,), ()),
    ((4, 4), (4,), ()),
)


NT = (((1,), (1,)), ((), ()))


def product(left, right):
    return (left.astype(F32) * right.astype(F32)).astype(BF)


def kernel(
    factor, scale,
    block_in, out_cot, conv_one, conv_two, filter_one, filter_two, w_in, w_out,
    fwd, inv, line, line_back, turn,
    in_grad, in_ref, out_ref, filter_one_grad, filter_two_grad,
    weights, grad_in, value_grad, gate_one_grad, gate_two_grad, second_out, gate_one_all,
    pieces_out, pieces_in, backs_out, backs_in, wide, narrow,
    left, left_peer, right_peer, own, got, sums, parts, last,
    weight_sems, wave_send, wave_recv, wave_own, pair_sems, send_sems, recv_sems, final_sems,
    greet_sems,
):
    at = coordinates()
    core = at["core"]
    partner = device_at(moved(at, "core", 1))
    around = {d: [device_at(moved(at, d, k)) for k in (1, 2, 3)] for d in "xyz"}
    refs = (fwd, inv, line, line_back, turn)
    copies = []

    def greet(sem, devices):
        for device in devices:
            pl.semaphore_signal(sem, inc=1, device_id=device, device_id_type=MESH)

    def remote(src, dst, send_sem, recv_sem, device):
        copy = pltpu.make_async_remote_copy(
            src_ref=src, dst_ref=dst, send_sem=send_sem, recv_sem=recv_sem,
            device_id=device, device_id_type=MESH,
        )
        copy.start()
        copies.append(copy)
        return copy

    barrier = pltpu.get_barrier_semaphore()
    near = [partner] + around["x"] + around["y"] + around["z"]
    greet(barrier, near)

    loads = []
    for k in (1, 2, 3, 0):
        src = w_out if k == 3 else w_in.at[:, pl.ds(k * 1024, 1024)]
        loads.append(pltpu.make_async_copy(src, weights.at[k], weight_sems.at[k]))
        loads[-1].start()

    def put_pieces(wave, j, one, two):
        both = [part.astype(F32).T.reshape(32, CH, LANES) for part in (one, two)]
        pieces_out[wave, pl.ds(32 * j, 32)] = jnp.concatenate(both, axis=1).astype(BF)

    def columns(j):
        return slice(256 * j, 256 * j + 256)

    for j in range(4):
        put_pieces(0, j, conv_one[:, columns(j)], filter_two[:, columns(j)])
    pl.semaphore_wait(barrier, len(near))
    greet(greet_sems.at[0], around["x"])
    for load in loads[:3]:
        load.wait()
    for j in range(4):
        c = columns(j)
        gate_one = jnp.dot(block_in[...], weights[1, :, c], preferred_element_type=F32).astype(BF)
        gate_two = jnp.dot(block_in[...], weights[2, :, c], preferred_element_type=F32).astype(BF)
        grad_second = lax.dot_general(
            out_cot[...], weights[3, c, :], NT, preferred_element_type=F32
        ).astype(BF)
        gate_two_grad[:, c] = product(grad_second, conv_two[:, c])
        second_out[:, c] = product(gate_two, conv_two[:, c])
        put_pieces(1, j, gate_one, product(grad_second, gate_two))
        if j == 1:
            pl.semaphore_wait(greet_sems.at[0], 3)
            greet(greet_sems.at[1], around["y"])
    pl.semaphore_wait(greet_sems.at[1], 3)
    greet(greet_sems.at[2], [partner])
    loads[3].wait()
    for j in range(2):
        value = jnp.dot(block_in[...], weights[0, :, columns(j)], preferred_element_type=F32)
        put_pieces(2, j, filter_one[:, columns(j)], value.astype(BF))
    pl.semaphore_wait(greet_sems.at[2], 1)

    def send(k, src, dst):
        send_wave(src, dst, wave_send.at[k], wave_recv.at[k], wave_own.at[k])

    send(0, pieces_out.at[0], pieces_in.at[0])
    send(1, pieces_out.at[1], pieces_in.at[1])
    for j in range(2, 4):
        value = jnp.dot(block_in[...], weights[0, :, columns(j)], preferred_element_type=F32)
        put_pieces(2, j, filter_one[:, columns(j)], value.astype(BF))
    send(2, pieces_out.at[2], pieces_in.at[2])

    theirs = pl.ds(pl.multiple_of((1 - core) * HALF, HALF), HALF)
    rights = (value_grad, gate_one_grad, gate_two_grad, out_cot)

    def pair_up(k, src, dst):
        return remote(src, dst, pair_sems.at[0, k], pair_sems.at[1, k], partner)

    def pair_right(block):
        return pair_up(block, rights[block].at[:, theirs], right_peer.at[block])

    def start_unit(u):
        group = UNITS[u][1]
        dim = ORDERS[group][0]
        for step in (2, 1, 3, 0):
            index = rows_at(0, group, (at[dim] + step) % 4)
            col = 0
            for which, block, first, width in SHARES[UNITS[u]]:
                rows = left[(which,) + index].reshape(256, 256)
                cols = pl.ds(pl.multiple_of(core * HALF + first, 128), width)
                right = jnp.concatenate(
                    [rights[block][:, cols], right_peer[block, :, first : first + width]], axis=0
                )
                own[u][step, ..., col : col + width] = (
                    jnp.dot(rows, right, preferred_element_type=F32)
                    .astype(BF)
                    .reshape(SUMMED[group][0] + (16, width))
                )
                col += width
            if step:
                remote(
                    own[u].at[step], got[u][0].at[step - 1], send_sems.at[u, 0, step - 1],
                    recv_sems.at[u, 0, step - 1], device_at(moved(at, dim, step)),
                )

    def advance(u, phase):
        group = UNITS[u][1]
        base = own[u].at[0] if phase == 0 else sums[u][phase - 1]
        index = () if phase == 0 else rows_at(phase, group, at[ORDERS[group][phase]])
        total = base[index + (Ellipsis,)].astype(F32)
        for k in range(3):
            pltpu.make_async_copy(
                got[u][phase].at[k], got[u][phase].at[k], recv_sems.at[u, phase, k]
            ).wait()
            total = total + got[u][phase][k].astype(F32)
        if phase == 2:
            parts[u][...] = (total * scale).reshape(2, 8, width_of(UNITS[u]))
            remote(parts[u].at[1 - core], last[u], final_sems.at[0, u], final_sems.at[1, u], partner)
            return
        sums[u][phase][...] = total.astype(BF)
        dim = ORDERS[group][phase + 1]
        for step in (2, 1, 3):
            index = rows_at(phase + 1, group, (at[dim] + step) % 4)
            remote(
                sums[u][phase].at[index], got[u][phase + 1].at[step - 1],
                send_sems.at[u, phase + 1, step - 1], recv_sems.at[u, phase + 1, step - 1],
                device_at(moved(at, dim, step)),
            )

    def finish(u):
        pltpu.make_async_copy(last[u], last[u], final_sems.at[1, u]).wait()
        col = 0
        for which, block, first, width in SHARES[UNITS[u]]:
            target, start = (out_ref, 0) if which else (in_ref, block * 2 * HALF)
            for part, half in ((parts[u].at[core], core), (last[u], 1 - core)):
                cols = pl.ds(pl.multiple_of(start + half * HALF + first, 128), width)
                target[:, cols] = part[:, col : col + width]
            col += width

    def add_in_grad(grad, block):
        for j in range(4):
            part = lax.dot_general(
                grad[...], weights[block, columns(j), :], NT, preferred_element_type=F32
            )
            grad_in[:, columns(j)] = part if block == 2 else grad_in[:, columns(j)] + part

    pairs = [
        pair_up(4, block_in, left_peer.at[0]),
        pair_up(5, second_out, left_peer.at[1]),
        pair_right(2),
        pair_right(3),
    ]
    shape = (2, 4, 4, 2, 16, 128)
    for k, ref in enumerate((block_in, second_out)):
        left[k, :, :, :, :, :, :128] = ref[...].T.reshape(shape)
    for copy in pairs:
        copy.wait_recv()
    for k in range(2):
        left[k, :, :, :, :, :, 128:] = left_peer[k].T.reshape(shape)
    for u in range(3):
        start_unit(u)
    add_in_grad(gate_two_grad, 2)

    def receive(k):
        wait_wave(pieces_out.at[k], pieces_in.at[k], wave_recv.at[k], wave_own.at[k])
        wide[k] = pieces_in[k].astype(F32).reshape(DEV * WAVE, LANES)

    def pull(field, c):
        start = field % 2 * CH + c
        return jnp.concatenate(
            [wide[field // 2, pl.ds(start + h, DEV, WAVE), :] for h in range(2)], axis=1
        )

    def push(field, c, data):
        for h in range(2):
            narrow[field // 2, pl.ds(field % 2 * CH + c + h, DEV, WAVE), :] = data[
                :, h * 128 : h * 128 + 128
            ]

    def first(i, carry):
        c = 2 * i
        gate, conv = pull(GATE_ONE, c), pull(CONV_ONE, c)
        first_out = round_mul(gate, conv)
        grad_first, filter_two_part = correlations(
            pull(GRAD_CONV_TWO, c),
            jnp.concatenate([pull(FILTER_TWO, c), first_out], axis=0),
            refs,
            factor,
        )
        push(GRAD_GATE_ONE, c, round_mul(grad_first, conv))
        push(FILTER_TWO_GRAD, c, filter_two_part)
        gate_one_all[i] = round_mul(grad_first, gate)
        return carry

    def second(i, carry):
        c = 2 * i
        grad_value, filter_one_part = correlations(
            gate_one_all[i],
            jnp.concatenate([pull(FILTER_ONE, c), pull(VALUE, c)], axis=0),
            refs,
            factor,
        )
        push(GRAD_VALUE, c, grad_value)
        push(FILTER_ONE_GRAD, c, filter_one_part)
        return carry

    def send_back(k):
        backs_out[k] = narrow[k].astype(BF).reshape(DEV, WAVE, LANES)
        send(3 + k, backs_out.at[k], backs_in.at[k])

    def take_back(k, one, two):
        wait_wave(backs_out.at[k], backs_in.at[k], wave_recv.at[3 + k], wave_own.at[3 + k])
        for j in range(4):
            part = backs_in[k, pl.ds(32 * j, 32)].astype(F32)
            one[:, columns(j)] = part[:, :CH].reshape(256, LANES).T.astype(BF)
            two[:, columns(j)] = part[:, CH:].reshape(256, LANES).T.astype(BF)

    receive(0)
    receive(1)
    lax.fori_loop(0, CH // 2, first, 0)
    send_back(0)
    for u in range(3):
        advance(u, 0)
    receive(2)
    lax.fori_loop(0, CH // 2, second, 0)
    send_back(1)
    for u in range(3):
        advance(u, 1)
    take_back(0, gate_one_grad, filter_two_grad)
    pair_right(1).wait_recv()
    for u in range(3, 6):
        start_unit(u)
    for u in range(3):
        advance(u, 2)
    add_in_grad(gate_one_grad, 1)
    take_back(1, value_grad, filter_one_grad)
    pair_right(0).wait_recv()
    for u in range(6, 9):
        start_unit(u)
    for u in range(3, 6):
        advance(u, 0)
    add_in_grad(value_grad, 0)
    in_grad[...] = grad_in[...].astype(BF)
    for u in range(3):
        finish(u)
    for u in range(6, 9):
        advance(u, 0)
    for phase in (1, 2):
        for u in range(3, 9):
            advance(u, phase)
    for u in range(3, 9):
        finish(u)
    for k in range(5):
        out, into = (pieces_out, pieces_in) if k < 3 else (backs_out, backs_in)
        wait_wave(out.at[k % 3], into.at[k % 3], wave_send.at[k])
    for copy in copies:
        copy.wait_send()


def shards(block_in, out_cot, w_in, w_out, conv_one, conv_two, filter_one, filter_two):
    rows, width = block_in.shape
    seq_len = rows * DEV
    scale = seq_len ** (-0.5)
    factor = scale / (2.0 * seq_len)
    tables = [jnp.asarray(t) for t in dft_tables()]
    own, got, sums, parts, last = [], [], [], [], []
    for unit in UNITS:
        w = width_of(unit)
        shapes = [shape + (16, w) for shape in SUMMED[unit[1]]]
        own.append(pltpu.VMEM((4,) + shapes[0], BF))
        got.append([pltpu.VMEM((3,) + shape, BF) for shape in shapes])
        sums.append([pltpu.VMEM(shape, BF) for shape in shapes[:2]])
        parts.append(pltpu.VMEM((2, 8, w), F32))
        last.append(pltpu.VMEM((8, w), F32))
    vmem = pl.BlockSpec(memory_space=pltpu.VMEM)
    anywhere = pl.BlockSpec(memory_space=pl.ANY)
    wave = (DEV, WAVE, LANES)
    flat = (DEV * WAVE, LANES)
    local = jax.ShapeDtypeStruct((rows, width), BF)
    dma = pltpu.SemaphoreType.DMA
    units = len(UNITS)
    return pl.pallas_call(
        functools.partial(kernel, factor, scale),
        out_shape=(
            local,
            jax.ShapeDtypeStruct((width // DEV, 3 * width), F32),
            jax.ShapeDtypeStruct((width // DEV, width), F32),
            local,
            local,
        ),
        in_specs=[vmem] * 6 + [anywhere] * 2 + [vmem] * 5,
        out_specs=(vmem,) * 5,
        scratch_shapes=[
            pltpu.VMEM((4, width, width), BF),
            pltpu.VMEM((rows, width), F32),
            pltpu.VMEM((rows, width), BF),
            pltpu.VMEM((rows, width), BF),
            pltpu.VMEM((rows, width), BF),
            pltpu.VMEM((rows, width), BF),
            pltpu.VMEM((CH // 2, DEV, 256), F32),
            pltpu.VMEM((3,) + wave, BF),
            pltpu.VMEM((3,) + wave, BF),
            pltpu.VMEM((2,) + wave, BF),
            pltpu.VMEM((2,) + wave, BF),
            pltpu.VMEM((3,) + flat, F32),
            pltpu.VMEM((2,) + flat, F32),
            pltpu.VMEM((2, 2, 4, 4, 2, 16, 256), BF),
            pltpu.VMEM((2, rows, width), BF),
            pltpu.VMEM((4, rows, HALF), BF),
            own, got, sums, parts, last,
            dma((4,)),
            dma((5,)),
            dma((5,)),
            dma((5,)),
            dma((2, 6)),
            dma((units, 3, 3)),
            dma((units, 3, 3)),
            dma((2, units)),
            pltpu.SemaphoreType.REGULAR((3,)),
        ],
        compiler_params=pltpu.CompilerParams(
            vmem_limit_bytes=60 << 20, collective_id=0, has_side_effects=True
        ),
        name="hyena_backward",
    )(block_in, out_cot, conv_one, conv_two, filter_one, filter_two, w_in, w_out, *tables)


def solution(mesh):
    rows = P(AXES, None)
    return jax.shard_map(
        shards,
        mesh=mesh,
        in_specs=(rows, rows, P(), P(), rows, rows, rows, rows),
        out_specs=(rows,) * 5,
        check_vma=False,
    )
```

```python
import functools

import jax
import jax.numpy as jnp
import numpy as np
from jax import lax
from jax.experimental import pallas as pl
from jax.experimental.pallas import tpu as pltpu
from jax.sharding import PartitionSpec as P

AXES = ("major", "minor")
DEV = 128
CH = 8
LANES = 128
BF = jnp.bfloat16
F32 = jnp.float32
CONV_ONE, FILTER_TWO, GATE_ONE, GRAD_CONV_TWO, FILTER_ONE, VALUE = range(6)
GRAD_GATE_ONE, FILTER_TWO_GRAD, GRAD_VALUE, FILTER_ONE_GRAD = range(4)
FIELDS_IN = 6
EARLY = True
UNROLL = 1
RINGS = 6
FIRST_AFTER = 1
FIELDS_OUT = 4
WAVE = 2 * CH
MESH = pl.DeviceIdType.MESH


def dft_tables():
    k1 = np.arange(256)[:, None]
    n1 = np.arange(128)[None, :]
    a = 2.0 * np.pi * ((k1 * n1) % 256) / 256
    c, s = np.cos(a), np.sin(a)
    n2 = np.arange(128)
    b = 2.0 * np.pi * ((n2[:, None] * n2[None, :]) % 128) / 128
    cb, sb = np.cos(b), np.sin(b)
    t = 2.0 * np.pi * (k1 * n2[None, :]) / 32768
    return (
        np.block([[c, -s], [-s, -c]]).astype(BF),
        np.block([[c.T, -s.T], [s.T, c.T]]).astype(BF),
        np.block([[cb, -sb], [sb, cb]]).astype(BF),
        np.block([[cb, sb], [-sb, cb]]).astype(BF),
        np.stack([np.cos(t), np.sin(t)]).astype(np.float32),
    )


def round_mul(a, b):
    return (a * b).astype(BF).astype(F32)


def spectrum_of(data, table, line, tw_re, tw_im):
    grid = jnp.dot(table, data, preferred_element_type=F32)
    out = []
    for h in range(2):
        re = grid[:256, h * 128 : h * 128 + 128]
        im = grid[256:, h * 128 : h * 128 + 128]
        turned = jnp.concatenate([re * tw_re + im * tw_im, im * tw_re - re * tw_im], axis=1)
        out.append(jnp.dot(turned.astype(BF), line, preferred_element_type=F32))
    return out


def correlations(left, pair, refs, factor):
    fwd, inv, line, line_back, turn = refs
    tw_re, tw_im = turn[0], turn[1]
    specs = spectrum_of(left.astype(BF), fwd[:, :128], line[...], tw_re, tw_im)
    packs = spectrum_of(pair.astype(BF), fwd[...], line[...], tw_re, tw_im)
    backs_re, backs_im = [], []
    for spec, pack in zip(specs, packs):
        l_re, l_im = spec[:, :128], spec[:, 128:]
        p_re, p_im = pack[:, :128], pack[:, 128:]
        both = jnp.concatenate([l_re * p_re + l_im * p_im, l_im * p_re - l_re * p_im], axis=1)
        back = jnp.dot(both.astype(BF), line_back[...], preferred_element_type=F32)
        b_re, b_im = back[:, :128], back[:, 128:]
        backs_re.append(b_re * tw_re - b_im * tw_im)
        backs_im.append(b_re * tw_im + b_im * tw_re)
    stacked = jnp.concatenate(
        [jnp.concatenate(backs_re, axis=1), jnp.concatenate(backs_im, axis=1)], axis=0
    ).astype(BF)
    out = jnp.dot(inv[...], stacked, preferred_element_type=F32) * factor
    return out[:128].astype(BF).astype(F32), out[128:].astype(BF).astype(F32)


def peer_of(step):
    rem, div = lax.rem, lax.div
    step = rem(step * 37, DEV)
    major, minor = lax.axis_index("major"), lax.axis_index("minor")
    x = rem(rem(div(minor, 2), 2) * 2 + div(major, 4) + div(step, 2), 4)
    y = rem(rem(major, 4) + div(step, 8), 4)
    z = rem(div(minor, 4) + div(step, 32), 4)
    core = rem(minor + step, 2)
    return (rem(x, 2) * 4 + y, z * 4 + div(x, 2) * 2 + core)


def my_index():
    return lax.axis_index("major") * 16 + lax.axis_index("minor")


def send_wave(src, dst, send_sem, recv_sem, own_sem):
    me = my_index()
    pltpu.make_async_copy(src.at[me], dst.at[me], own_sem).start()

    def send(step, carry):
        major, minor = peer_of(step)
        pltpu.make_async_remote_copy(
            src_ref=src.at[major * 16 + minor],
            dst_ref=dst.at[me],
            send_sem=send_sem,
            recv_sem=recv_sem,
            device_id=(major, minor),
            device_id_type=MESH,
        ).start()
        return carry

    lax.fori_loop(1, DEV, send, 0)


def wait_wave(src, dst, sem, own_sem=None):
    if own_sem is not None:
        me = my_index()
        pltpu.make_async_copy(src.at[me], dst.at[me], own_sem).wait()
    most = pl.ds(0, DEV - 1)
    pltpu.make_async_copy(src.at[most], dst.at[most], sem).wait()


HALF = 512
SHARES = {
    (0, 0): [(0, 2, 0, 256), (1, 3, 0, 128)],
    (0, 1): [(0, 2, 256, 128), (1, 3, 128, 256)],
    (0, 2): [(0, 2, 384, 128), (1, 3, 384, 128)],
    (1, 0): [(0, 1, 0, 128)],
    (1, 1): [(0, 1, 128, 128)],
    (1, 2): [(0, 1, 256, 256)],
    (2, 0): [(0, 0, 0, 256)],
    (2, 1): [(0, 0, 256, 128)],
    (2, 2): [(0, 0, 384, 128)],
}
ORDERS = (("y", "z", "x"), ("z", "x", "y"), ("x", "y", "z"))
UNITS = [(w, g) for w in range(3) for g in range(3)]


def width_of(unit):
    return sum(share[3] for share in SHARES[unit])


def coordinates():
    major, minor = lax.axis_index("major"), lax.axis_index("minor")
    x = (minor // 2) % 2 * 2 + major // 4
    return {"x": x, "y": major % 4, "z": minor // 4, "core": minor % 2}


def device_at(at):
    return (at["x"] % 2 * 4 + at["y"], at["z"] * 4 + at["x"] // 2 * 2 + at["core"])


def moved(at, dim, step):
    return dict(at, **{dim: (at[dim] + step) % (2 if dim == "core" else 4)})


def rows_at(phase, group, value):
    every = slice(None)
    if group == 0:
        return [(every, value), (every, value), (value % 2, value // 2)][phase]
    if group == 1:
        return [(every, every, value), (value % 2, every, value // 2), (value,)][phase]
    return [(value % 2, every, every, value // 2), (value,), (value,)][phase]


SUMMED = (
    ((2, 4, 2), (2, 2), ()),
    ((2, 4, 2), (4,), ()),
    ((4, 4), (4,), ()),
)


NT = (((1,), (1,)), ((), ()))


def product(left, right):
    return (left.astype(F32) * right.astype(F32)).astype(BF)


def kernel(
    factor, scale,
    block_in, out_cot, conv_one, conv_two, filter_one, filter_two, w_in, w_out,
    fwd, inv, line, line_back, turn,
    in_grad, in_ref, out_ref, filter_one_grad, filter_two_grad,
    weights, grad_in, value_grad, gate_one_grad, gate_two_grad, second_out, gate_one_all,
    pieces_out, pieces_in, backs_out, backs_in, wide, narrow,
    left, left_peer, right_peer, own, got, sums, parts, last,
    weight_sems, wave_send, wave_recv, wave_own, pair_sems, send_sems, recv_sems, final_sems,
    greet_sems,
):
    at = coordinates()
    core = at["core"]
    partner = device_at(moved(at, "core", 1))
    refs = (fwd, inv, line, line_back, turn)
    copies = []

    def greet(sem, devices):
        for device in devices:
            pl.semaphore_signal(sem, inc=1, device_id=device, device_id_type=MESH)

    def remote(src, dst, send_sem, recv_sem, device):
        copy = pltpu.make_async_remote_copy(
            src_ref=src, dst_ref=dst, send_sem=send_sem, recv_sem=recv_sem,
            device_id=device, device_id_type=MESH,
        )
        copy.start()
        copies.append(copy)
        return copy

    barrier = pltpu.get_barrier_semaphore()
    line_of = [moved(at, "x", k) for k in range(4)]
    line_of = line_of[1:] + [moved(one, "core", 1) for one in line_of]
    plane = [moved(moved(at, "y", j), "z", k) for j in range(4) for k in range(4) if j or k]
    plane = [device_at(one) for one in plane]
    near = plane + [device_at(one) for one in line_of]
    greet(barrier, near)

    loads = []
    for k in (1, 2, 3, 0):
        src = w_out if k == 3 else w_in.at[:, pl.ds(k * 1024, 1024)]
        loads.append(pltpu.make_async_copy(src, weights.at[k], weight_sems.at[k]))
        loads[-1].start()

    def put_pieces(wave, j, one, two):
        both = [part.astype(F32).T.reshape(32, CH, LANES) for part in (one, two)]
        pieces_out[wave, pl.ds(32 * j, 32)] = jnp.concatenate(both, axis=1).astype(BF)

    def columns(j):
        return slice(256 * j, 256 * j + 256)

    def send(k, src, dst):
        send_wave(src, dst, wave_send.at[k], wave_recv.at[k], wave_own.at[k])

    for j in range(4):
        put_pieces(0, j, conv_one[:, columns(j)], filter_two[:, columns(j)])
    pl.semaphore_wait(barrier, len(near))
    greet(greet_sems.at[0], plane)
    for load in loads[:3]:
        load.wait()
    for j in range(4):
        c = columns(j)
        gate_one = jnp.dot(block_in[...], weights[1, :, c], preferred_element_type=F32).astype(BF)
        gate_two = jnp.dot(block_in[...], weights[2, :, c], preferred_element_type=F32).astype(BF)
        grad_second = lax.dot_general(
            out_cot[...], weights[3, c, :], NT, preferred_element_type=F32
        ).astype(BF)
        gate_two_grad[:, c] = product(grad_second, conv_two[:, c])
        second_out[:, c] = product(gate_two, conv_two[:, c])
        put_pieces(1, j, gate_one, product(grad_second, gate_two))
        if j == FIRST_AFTER:
            pl.semaphore_wait(greet_sems.at[0], len(plane))
            send(0, pieces_out.at[0], pieces_in.at[0])
    send(1, pieces_out.at[1], pieces_in.at[1])
    loads[3].wait()
    for j in range(4):
        value = jnp.dot(block_in[...], weights[0, :, columns(j)], preferred_element_type=F32)
        put_pieces(2, j, filter_one[:, columns(j)], value.astype(BF))
    send(2, pieces_out.at[2], pieces_in.at[2])

    theirs = pl.ds(pl.multiple_of((1 - core) * HALF, HALF), HALF)
    rights = (value_grad, gate_one_grad, gate_two_grad, out_cot)

    def pair_up(k, src, dst):
        return remote(src, dst, pair_sems.at[0, k], pair_sems.at[1, k], partner)

    def pair_right(block):
        return pair_up(block, rights[block].at[:, theirs], right_peer.at[block])

    def start_unit(u):
        group = UNITS[u][1]
        dim = ORDERS[group][0]
        for step in (2, 1, 3, 0):
            index = rows_at(0, group, (at[dim] + step) % 4)
            col = 0
            for which, block, first, width in SHARES[UNITS[u]]:
                rows = left[(which,) + index].reshape(256, 256)
                cols = pl.ds(pl.multiple_of(core * HALF + first, 128), width)
                right = jnp.concatenate(
                    [rights[block][:, cols], right_peer[block, :, first : first + width]], axis=0
                )
                own[u][step, ..., col : col + width] = (
                    jnp.dot(rows, right, preferred_element_type=F32)
                    .astype(BF)
                    .reshape(SUMMED[group][0] + (16, width))
                )
                col += width

    def halves(u):
        count = SUMMED[UNITS[u][1]][0][0] // 2
        return pl.ds(0, count), pl.ds(count, count)

    def send_unit(u):
        dim = ORDERS[UNITS[u][1]][0]
        if u >= RINGS:
            for step in (2, 1, 3):
                remote(
                    own[u].at[step], got[u][0].at[step - 1], send_sems.at[u, 0, step - 1],
                    recv_sems.at[u, 0, step - 1], device_at(moved(at, dim, step)),
                )
            return
        low, high = halves(u)
        for k, (step, rows, to, slot) in enumerate(
            ((2, low, 1, 1), (2, high, 3, 1), (1, high, 1, 0), (3, low, 3, 2))
        ):
            remote(
                own[u].at[step, rows], got[u][0].at[slot, rows], send_sems.at[u, 0, k],
                recv_sems.at[u, 0, k], device_at(moved(at, dim, to)),
            )

    def pass_on(u):
        dim = ORDERS[UNITS[u][1]][0]
        low, high = halves(u)
        for k, (step, rows) in enumerate(((1, low), (3, high))):
            came = got[u][0].at[1, rows]
            pltpu.make_async_copy(came, came, recv_sems.at[u, 0, k]).wait()
            mine = own[u][step, rows].astype(F32) + came[...].astype(F32)
            own[u][step, rows] = mine.astype(BF)
            remote(
                own[u].at[step, rows], got[u][0].at[step - 1, rows], send_sems.at[u, 0, 4 + k],
                recv_sems.at[u, 0, 4 + k], device_at(moved(at, dim, step)),
            )

    def advance(u, phase):
        group = UNITS[u][1]
        base = own[u].at[0] if phase == 0 else sums[u]
        index = () if phase == 0 else rows_at(phase, group, at[ORDERS[group][phase]])
        total = base[index + (Ellipsis,)].astype(F32)
        if phase == 0 and u < RINGS:
            low, high = halves(u)
            for k, slot, rows in ((2, 0, high), (3, 2, low), (4, 0, low), (5, 2, high)):
                came = got[u][0].at[slot, rows]
                pltpu.make_async_copy(came, came, recv_sems.at[u, 0, k]).wait()
            total = total + got[u][0][0].astype(F32) + got[u][0][2].astype(F32)
        else:
            for k in range(3):
                came = got[u][phase].at[k]
                pltpu.make_async_copy(came, came, recv_sems.at[u, phase, k]).wait()
                total = total + came[...].astype(F32)
        dim = ORDERS[group][phase + 1]
        if phase == 0:
            sums[u][...] = total.astype(BF)
            for step in (2, 1, 3):
                index = rows_at(1, group, (at[dim] + step) % 4)
                remote(
                    sums[u].at[index], got[u][1].at[step - 1], send_sems.at[u, 1, step - 1],
                    recv_sems.at[u, 1, step - 1], device_at(moved(at, dim, step)),
                )
            return
        parts[u][...] = total.reshape(SUMMED[group][1] + (2, 8, width_of(UNITS[u])))
        for step in (2, 1, 3, 0):
            index = rows_at(2, group, (at[dim] + step) % 4)
            there = moved(at, dim, step)
            for flip in (0, 1):
                if step or flip:
                    to = moved(there, "core", flip)
                    remote(
                        parts[u].at[index + (to["core"],)], last[u].at[core * 4 + step],
                        final_sems.at[0, u, 2 * step + flip], final_sems.at[1, u, 0], device_at(to),
                    )
        index = rows_at(2, group, at[dim])
        last[u][core * 4] = parts[u][index + (core,)]

    def finish(u):
        most = pl.ds(0, 7)
        pltpu.make_async_copy(last[u].at[most], last[u].at[most], final_sems.at[1, u, 0]).wait()
        for half in range(2):
            total = last[u][4 * half]
            for k in range(1, 4):
                total = total + last[u][4 * half + k]
            total = total * scale
            col = 0
            for which, block, first, width in SHARES[UNITS[u]]:
                target, start = (out_ref, 0) if which else (in_ref, block * 2 * HALF)
                cols = slice(start + half * HALF + first, start + half * HALF + first + width)
                target[:, cols] = total[:, col : col + width]
                col += width

    def add_in_grad(grad, block):
        for j in range(4):
            part = lax.dot_general(
                grad[...], weights[block, columns(j), :], NT, preferred_element_type=F32
            )
            grad_in[:, columns(j)] = part if block == 2 else grad_in[:, columns(j)] + part

    pairs = [
        pair_up(4, block_in, left_peer.at[0]),
        pair_up(5, second_out, left_peer.at[1]),
        pair_right(2),
        pair_right(3),
    ]
    shape = (2, 4, 4, 2, 16, 128)
    for k, ref in enumerate((block_in, second_out)):
        left[k, :, :, :, :, :, :128] = ref[...].T.reshape(shape)
    for copy in pairs:
        copy.wait_recv()
    for k in range(2):
        left[k, :, :, :, :, :, 128:] = left_peer[k].T.reshape(shape)
    for u in range(3):
        start_unit(u)
    if EARLY:
        for u in range(3):
            send_unit(u)
    add_in_grad(gate_two_grad, 2)

    def receive(k):
        wait_wave(pieces_out.at[k], pieces_in.at[k], wave_recv.at[k], wave_own.at[k])
        wide[k] = pieces_in[k].astype(F32).reshape(DEV * WAVE, LANES)

    def pull(field, c):
        start = field % 2 * CH + c
        return jnp.concatenate(
            [wide[field // 2, pl.ds(start + h, DEV, WAVE), :] for h in range(2)], axis=1
        )

    def push(field, c, data):
        for h in range(2):
            narrow[field // 2, pl.ds(field % 2 * CH + c + h, DEV, WAVE), :] = data[
                :, h * 128 : h * 128 + 128
            ]

    def first(i, carry):
        c = 2 * i
        gate, conv = pull(GATE_ONE, c), pull(CONV_ONE, c)
        first_out = round_mul(gate, conv)
        grad_first, filter_two_part = correlations(
            pull(GRAD_CONV_TWO, c),
            jnp.concatenate([pull(FILTER_TWO, c), first_out], axis=0),
            refs,
            factor,
        )
        push(GRAD_GATE_ONE, c, round_mul(grad_first, conv))
        push(FILTER_TWO_GRAD, c, filter_two_part)
        gate_one_all[i] = round_mul(grad_first, gate)
        return carry

    def second(i, carry):
        c = 2 * i
        grad_value, filter_one_part = correlations(
            gate_one_all[i],
            jnp.concatenate([pull(FILTER_ONE, c), pull(VALUE, c)], axis=0),
            refs,
            factor,
        )
        push(GRAD_VALUE, c, grad_value)
        push(FILTER_ONE_GRAD, c, filter_one_part)
        return carry

    def send_back(k):
        backs_out[k] = narrow[k].astype(BF).reshape(DEV, WAVE, LANES)
        send(3 + k, backs_out.at[k], backs_in.at[k])

    def wait_back(k):
        wait_wave(backs_out.at[k], backs_in.at[k], wave_recv.at[3 + k], wave_own.at[3 + k])

    def take_back(field, result):
        start = field % 2 * CH
        for j in range(4):
            part = backs_in[field // 2, pl.ds(32 * j, 32)].astype(F32)[:, start : start + CH]
            result[:, columns(j)] = part.reshape(256, LANES).T.astype(BF)

    receive(0)
    receive(1)
    if not EARLY:
        for u in range(3):
            send_unit(u)
    lax.fori_loop(0, CH // 2, first, 0, unroll=UNROLL)
    send_back(0)
    for u in range(min(3, RINGS)):
        pass_on(u)
    receive(2)
    lax.fori_loop(0, CH // 2, second, 0, unroll=UNROLL)
    send_back(1)
    for u in range(3):
        advance(u, 0)
    wait_back(0)
    take_back(GRAD_GATE_ONE, gate_one_grad)
    pair_right(1).wait_recv()
    for u in range(3, 6):
        start_unit(u)
        send_unit(u)
    for u in range(3):
        advance(u, 1)
    add_in_grad(gate_one_grad, 1)
    wait_back(1)
    take_back(GRAD_VALUE, value_grad)
    pair_right(0).wait_recv()
    for u in range(6, 9):
        start_unit(u)
        send_unit(u)
    for u in range(3, min(6, RINGS)):
        pass_on(u)
    add_in_grad(value_grad, 0)
    in_grad[...] = grad_in[...].astype(BF)
    for u in range(3, 6):
        advance(u, 0)
    for u in range(6, RINGS):
        pass_on(u)
    for u in range(6, 9):
        advance(u, 0)
    for u in range(3, 6):
        advance(u, 1)
    for u in range(3):
        finish(u)
    take_back(FILTER_TWO_GRAD, filter_two_grad)
    for u in range(6, 9):
        advance(u, 1)
    for u in range(3, 6):
        finish(u)
    take_back(FILTER_ONE_GRAD, filter_one_grad)
    for u in range(6, 9):
        finish(u)
    for k in range(3):
        wait_wave(pieces_out.at[k], pieces_in.at[k], wave_send.at[k])
    for k in range(2):
        wait_wave(backs_out.at[k], backs_in.at[k], wave_send.at[3 + k])
    for copy in copies:
        copy.wait_send()


def store_kernel(*refs):
    for src, dst in zip(refs[:5], refs[5:]):
        dst[...] = src[...]


def shards(block_in, out_cot, w_in, w_out, conv_one, conv_two, filter_one, filter_two):
    rows, width = block_in.shape
    seq_len = rows * DEV
    scale = seq_len ** (-0.5)
    factor = scale / (2.0 * seq_len)
    tables = [jnp.asarray(t) for t in dft_tables()]
    own, got, sums, parts, last = [], [], [], [], []
    for unit in UNITS:
        w = width_of(unit)
        first, second, _ = SUMMED[unit[1]]
        own.append(pltpu.VMEM((4,) + first + (16, w), BF))
        got.append([pltpu.VMEM((3,) + shape + (16, w), BF) for shape in (first, second)])
        sums.append(pltpu.VMEM(first + (16, w), BF))
        parts.append(pltpu.VMEM(second + (2, 8, w), F32))
        last.append(pltpu.VMEM((8, 8, w), F32))
    vmem = pl.BlockSpec(memory_space=pltpu.VMEM)
    anywhere = pl.BlockSpec(memory_space=pl.ANY)
    wave = (DEV, WAVE, LANES)
    flat = (DEV * WAVE, LANES)
    local = jax.ShapeDtypeStruct((rows, width), BF)
    dma = pltpu.SemaphoreType.DMA
    units = len(UNITS)
    outputs = (
        local,
        jax.ShapeDtypeStruct((width // DEV, 3 * width), F32),
        jax.ShapeDtypeStruct((width // DEV, width), F32),
        local,
        local,
    )
    results = pl.pallas_call(
        functools.partial(kernel, factor, scale),
        out_shape=outputs,
        in_specs=[vmem] * 6 + [anywhere] * 2 + [vmem] * 5,
        out_specs=(vmem,) * 5,
        scratch_shapes=[
            pltpu.VMEM((4, width, width), BF),
            pltpu.VMEM((rows, width), F32),
            pltpu.VMEM((rows, width), BF),
            pltpu.VMEM((rows, width), BF),
            pltpu.VMEM((rows, width), BF),
            pltpu.VMEM((rows, width), BF),
            pltpu.VMEM((CH // 2, DEV, 256), F32),
            pltpu.VMEM((3,) + wave, BF),
            pltpu.VMEM((3,) + wave, BF),
            pltpu.VMEM((2,) + wave, BF),
            pltpu.VMEM((2,) + wave, BF),
            pltpu.VMEM((3,) + flat, F32),
            pltpu.VMEM((2,) + flat, F32),
            pltpu.VMEM((2, 2, 4, 4, 2, 16, 256), BF),
            pltpu.VMEM((2, rows, width), BF),
            pltpu.VMEM((4, rows, HALF), BF),
            own, got, sums, parts, last,
            dma((4,)),
            dma((5,)),
            dma((5,)),
            dma((5,)),
            dma((2, 6)),
            dma((units, 2, 6)),
            dma((units, 2, 6)),
            dma((2, units, 8)),
            pltpu.SemaphoreType.REGULAR((1,)),
        ],
        compiler_params=pltpu.CompilerParams(
            vmem_limit_bytes=60 << 20, collective_id=0, has_side_effects=True
        ),
        name="hyena_backward",
    )(block_in, out_cot, conv_one, conv_two, filter_one, filter_two, w_in, w_out, *tables)
    return pl.pallas_call(
        store_kernel,
        out_shape=outputs,
        in_specs=[vmem] * 5,
        out_specs=(vmem,) * 5,
        name="store",
    )(*results)


def solution(mesh):
    rows = P(AXES, None)
    return jax.shard_map(
        shards,
        mesh=mesh,
        in_specs=(rows, rows, P(), P(), rows, rows, rows, rows),
        out_specs=(rows,) * 5,
        check_vma=False,
    )
```

```python
import functools

import jax
import jax.numpy as jnp
import numpy as np
from jax import lax
from jax.experimental import pallas as pl
from jax.experimental.pallas import tpu as pltpu
from jax.sharding import PartitionSpec as P

AXES = ("major", "minor")
DEV = 128
CH = 8
LANES = 128
BF = jnp.bfloat16
F32 = jnp.float32
CONV_ONE, FILTER_TWO, GATE_ONE, GRAD_CONV_TWO, FILTER_ONE, VALUE = range(6)
GRAD_GATE_ONE, FILTER_TWO_GRAD, GRAD_VALUE, FILTER_ONE_GRAD = range(4)
FIELDS_IN = 6
EARLY = True
UNROLL = 2
RINGS = 6
FIRST_AFTER = 2
NEAR_AFTER = 0
FIELDS_OUT = 4
WAVE = 2 * CH
MESH = pl.DeviceIdType.MESH


def dft_tables():
    k1 = np.arange(256)[:, None]
    n1 = np.arange(128)[None, :]
    a = 2.0 * np.pi * ((k1 * n1) % 256) / 256
    c, s = np.cos(a), np.sin(a)
    n2 = np.arange(128)
    b = 2.0 * np.pi * ((n2[:, None] * n2[None, :]) % 128) / 128
    cb, sb = np.cos(b), np.sin(b)
    t = 2.0 * np.pi * (k1 * n2[None, :]) / 32768
    return (
        np.block([[c, -s], [-s, -c]]).astype(BF),
        np.block([[c.T, -s.T], [s.T, c.T]]).astype(BF),
        np.block([[cb, -sb], [sb, cb]]).astype(BF),
        np.block([[cb, sb], [-sb, cb]]).astype(BF),
        np.stack([np.cos(t), np.sin(t)]).astype(np.float32),
    )


def round_mul(a, b):
    return (a * b).astype(BF).astype(F32)


def spectrum_of(data, table, line, tw_re, tw_im):
    grid = jnp.dot(table, data, preferred_element_type=F32)
    out = []
    for h in range(2):
        re = grid[:256, h * 128 : h * 128 + 128]
        im = grid[256:, h * 128 : h * 128 + 128]
        turned = jnp.concatenate([re * tw_re + im * tw_im, im * tw_re - re * tw_im], axis=1)
        out.append(jnp.dot(turned.astype(BF), line, preferred_element_type=F32))
    return out


def correlations(left, pair, refs, factor):
    fwd, inv, line, line_back, turn = refs
    tw_re, tw_im = turn[0], turn[1]
    specs = spectrum_of(left.astype(BF), fwd[:, :128], line[...], tw_re, tw_im)
    packs = spectrum_of(pair.astype(BF), fwd[...], line[...], tw_re, tw_im)
    backs_re, backs_im = [], []
    for spec, pack in zip(specs, packs):
        l_re, l_im = spec[:, :128], spec[:, 128:]
        p_re, p_im = pack[:, :128], pack[:, 128:]
        both = jnp.concatenate([l_re * p_re + l_im * p_im, l_im * p_re - l_re * p_im], axis=1)
        back = jnp.dot(both.astype(BF), line_back[...], preferred_element_type=F32)
        b_re, b_im = back[:, :128], back[:, 128:]
        backs_re.append(b_re * tw_re - b_im * tw_im)
        backs_im.append(b_re * tw_im + b_im * tw_re)
    stacked = jnp.concatenate(
        [jnp.concatenate(backs_re, axis=1), jnp.concatenate(backs_im, axis=1)], axis=0
    ).astype(BF)
    out = jnp.dot(inv[...], stacked, preferred_element_type=F32) * factor
    return out[:128].astype(BF).astype(F32), out[128:].astype(BF).astype(F32)


def peer_of(step):
    rem, div = lax.rem, lax.div
    step = rem(step * 37, DEV)
    major, minor = lax.axis_index("major"), lax.axis_index("minor")
    x = rem(rem(div(minor, 2), 2) * 2 + div(major, 4) + div(step, 2), 4)
    y = rem(rem(major, 4) + div(step, 8), 4)
    z = rem(div(minor, 4) + div(step, 32), 4)
    core = rem(minor + step, 2)
    return (rem(x, 2) * 4 + y, z * 4 + div(x, 2) * 2 + core)


def my_index():
    return lax.axis_index("major") * 16 + lax.axis_index("minor")


def send_wave(src, dst, send_sem, recv_sem, own_sem):
    me = my_index()
    pltpu.make_async_copy(src.at[me], dst.at[me], own_sem).start()

    def send(step, carry):
        major, minor = peer_of(step)
        pltpu.make_async_remote_copy(
            src_ref=src.at[major * 16 + minor],
            dst_ref=dst.at[me],
            send_sem=send_sem,
            recv_sem=recv_sem,
            device_id=(major, minor),
            device_id_type=MESH,
        ).start()
        return carry

    lax.fori_loop(1, DEV, send, 0)


def wait_wave(src, dst, sem, own_sem=None):
    if own_sem is not None:
        me = my_index()
        pltpu.make_async_copy(src.at[me], dst.at[me], own_sem).wait()
    most = pl.ds(0, DEV - 1)
    pltpu.make_async_copy(src.at[most], dst.at[most], sem).wait()


HALF = 512
SHARES = {
    (0, 0): [(0, 2, 0, 256), (1, 3, 0, 128)],
    (0, 1): [(0, 2, 256, 128), (1, 3, 128, 256)],
    (0, 2): [(0, 2, 384, 128), (1, 3, 384, 128)],
    (1, 0): [(0, 1, 0, 128)],
    (1, 1): [(0, 1, 128, 128)],
    (1, 2): [(0, 1, 256, 256)],
    (2, 0): [(0, 0, 0, 256)],
    (2, 1): [(0, 0, 256, 128)],
    (2, 2): [(0, 0, 384, 128)],
}
ORDERS = (("y", "z", "x"), ("z", "x", "y"), ("x", "y", "z"))
UNITS = [(w, g) for w in range(3) for g in range(3)]


def width_of(unit):
    return sum(share[3] for share in SHARES[unit])


def coordinates():
    major, minor = lax.axis_index("major"), lax.axis_index("minor")
    x = (minor // 2) % 2 * 2 + major // 4
    return {"x": x, "y": major % 4, "z": minor // 4, "core": minor % 2}


def device_at(at):
    return (at["x"] % 2 * 4 + at["y"], at["z"] * 4 + at["x"] // 2 * 2 + at["core"])


def moved(at, dim, step):
    return dict(at, **{dim: (at[dim] + step) % (2 if dim == "core" else 4)})


def rows_at(phase, group, value):
    every = slice(None)
    if group == 0:
        return [(every, value), (every, value), (value % 2, value // 2)][phase]
    if group == 1:
        return [(every, every, value), (value % 2, every, value // 2), (value,)][phase]
    return [(value % 2, every, every, value // 2), (value,), (value,)][phase]


SUMMED = (
    ((2, 4, 2), (2, 2), ()),
    ((2, 4, 2), (4,), ()),
    ((4, 4), (4,), ()),
)


NT = (((1,), (1,)), ((), ()))


def product(left, right):
    return (left.astype(F32) * right.astype(F32)).astype(BF)


def kernel(
    factor, scale,
    block_in, out_cot, conv_one, conv_two, filter_one, filter_two, w_in, w_out,
    fwd, inv, line, line_back, turn,
    in_grad, in_ref, out_ref, filter_one_grad, filter_two_grad,
    weights, grad_in, value_grad, gate_one_grad, gate_two_grad, second_out, gate_one_all,
    pieces_out, pieces_in, backs_out, backs_in, wide, narrow,
    left, left_peer, right_peer, own, got, sums, parts, last,
    weight_sems, wave_send, wave_recv, wave_own, pair_sems, send_sems, recv_sems, final_sems,
    greet_sems,
):
    at = coordinates()
    core = at["core"]
    partner = device_at(moved(at, "core", 1))
    refs = (fwd, inv, line, line_back, turn)
    copies = []

    def greet(sem, devices):
        for device in devices:
            pl.semaphore_signal(sem, inc=1, device_id=device, device_id_type=MESH)

    def remote(src, dst, send_sem, recv_sem, device):
        copy = pltpu.make_async_remote_copy(
            src_ref=src, dst_ref=dst, send_sem=send_sem, recv_sem=recv_sem,
            device_id=device, device_id_type=MESH,
        )
        copy.start()
        copies.append(copy)
        return copy

    barrier = pltpu.get_barrier_semaphore()
    line_of = [moved(at, "x", k) for k in range(4)]
    line_of = line_of[1:] + [moved(one, "core", 1) for one in line_of]
    plane = [moved(moved(at, "y", j), "z", k) for j in range(4) for k in range(4) if j or k]
    plane = [device_at(one) for one in plane]
    near = plane + [device_at(one) for one in line_of]
    greet(barrier, near)

    loads = []
    for k in (1, 2, 3, 0):
        src = w_out if k == 3 else w_in.at[:, pl.ds(k * 1024, 1024)]
        loads.append(pltpu.make_async_copy(src, weights.at[k], weight_sems.at[k]))
        loads[-1].start()

    def put_pieces(wave, j, one, two):
        both = [part.astype(F32).T.reshape(32, CH, LANES) for part in (one, two)]
        pieces_out[wave, pl.ds(32 * j, 32)] = jnp.concatenate(both, axis=1).astype(BF)

    def columns(j):
        return slice(256 * j, 256 * j + 256)

    def send(k, src, dst):
        send_wave(src, dst, wave_send.at[k], wave_recv.at[k], wave_own.at[k])

    for j in range(4):
        put_pieces(0, j, conv_one[:, columns(j)], filter_two[:, columns(j)])
    if NEAR_AFTER < 0:
        pl.semaphore_wait(barrier, len(near))
        greet(greet_sems.at[0], plane)
    for load in loads[:3]:
        load.wait()
    for j in range(4):
        c = columns(j)
        gate_one = jnp.dot(block_in[...], weights[1, :, c], preferred_element_type=F32).astype(BF)
        gate_two = jnp.dot(block_in[...], weights[2, :, c], preferred_element_type=F32).astype(BF)
        grad_second = lax.dot_general(
            out_cot[...], weights[3, c, :], NT, preferred_element_type=F32
        ).astype(BF)
        gate_two_grad[:, c] = product(grad_second, conv_two[:, c])
        second_out[:, c] = product(gate_two, conv_two[:, c])
        put_pieces(1, j, gate_one, product(grad_second, gate_two))
        if j == NEAR_AFTER:
            pl.semaphore_wait(barrier, len(near))
            greet(greet_sems.at[0], plane)
        if j == FIRST_AFTER:
            pl.semaphore_wait(greet_sems.at[0], len(plane))
            send(0, pieces_out.at[0], pieces_in.at[0])
    send(1, pieces_out.at[1], pieces_in.at[1])
    loads[3].wait()
    for j in range(4):
        value = jnp.dot(block_in[...], weights[0, :, columns(j)], preferred_element_type=F32)
        put_pieces(2, j, filter_one[:, columns(j)], value.astype(BF))
    send(2, pieces_out.at[2], pieces_in.at[2])

    theirs = pl.ds(pl.multiple_of((1 - core) * HALF, HALF), HALF)
    rights = (value_grad, gate_one_grad, gate_two_grad, out_cot)

    def pair_up(k, src, dst):
        return remote(src, dst, pair_sems.at[0, k], pair_sems.at[1, k], partner)

    def pair_right(block):
        return pair_up(block, rights[block].at[:, theirs], right_peer.at[block])

    def start_unit(u):
        group = UNITS[u][1]
        dim = ORDERS[group][0]
        for step in (2, 1, 3, 0):
            index = rows_at(0, group, (at[dim] + step) % 4)
            col = 0
            for which, block, first, width in SHARES[UNITS[u]]:
                rows = left[(which,) + index].reshape(256, 256)
                cols = pl.ds(pl.multiple_of(core * HALF + first, 128), width)
                right = jnp.concatenate(
                    [rights[block][:, cols], right_peer[block, :, first : first + width]], axis=0
                )
                own[u][step, ..., col : col + width] = (
                    jnp.dot(rows, right, preferred_element_type=F32)
                    .astype(BF)
                    .reshape(SUMMED[group][0] + (16, width))
                )
                col += width

    def halves(u):
        count = SUMMED[UNITS[u][1]][0][0] // 2
        return pl.ds(0, count), pl.ds(count, count)

    def send_unit(u):
        dim = ORDERS[UNITS[u][1]][0]
        if u >= RINGS:
            for step in (2, 1, 3):
                remote(
                    own[u].at[step], got[u][0].at[step - 1], send_sems.at[u, 0, step - 1],
                    recv_sems.at[u, 0, step - 1], device_at(moved(at, dim, step)),
                )
            return
        low, high = halves(u)
        for k, (step, rows, to, slot) in enumerate(
            ((2, low, 1, 1), (2, high, 3, 1), (1, high, 1, 0), (3, low, 3, 2))
        ):
            remote(
                own[u].at[step, rows], got[u][0].at[slot, rows], send_sems.at[u, 0, k],
                recv_sems.at[u, 0, k], device_at(moved(at, dim, to)),
            )

    def pass_on(u):
        dim = ORDERS[UNITS[u][1]][0]
        low, high = halves(u)
        for k, (step, rows) in enumerate(((1, low), (3, high))):
            came = got[u][0].at[1, rows]
            pltpu.make_async_copy(came, came, recv_sems.at[u, 0, k]).wait()
            mine = own[u][step, rows].astype(F32) + came[...].astype(F32)
            own[u][step, rows] = mine.astype(BF)
            remote(
                own[u].at[step, rows], got[u][0].at[step - 1, rows], send_sems.at[u, 0, 4 + k],
                recv_sems.at[u, 0, 4 + k], device_at(moved(at, dim, step)),
            )

    def advance(u, phase):
        group = UNITS[u][1]
        base = own[u].at[0] if phase == 0 else sums[u]
        index = () if phase == 0 else rows_at(phase, group, at[ORDERS[group][phase]])
        total = base[index + (Ellipsis,)].astype(F32)
        if phase == 0 and u < RINGS:
            low, high = halves(u)
            for k, slot, rows in ((2, 0, high), (3, 2, low), (4, 0, low), (5, 2, high)):
                came = got[u][0].at[slot, rows]
                pltpu.make_async_copy(came, came, recv_sems.at[u, 0, k]).wait()
            total = total + got[u][0][0].astype(F32) + got[u][0][2].astype(F32)
        else:
            for k in range(3):
                came = got[u][phase].at[k]
                pltpu.make_async_copy(came, came, recv_sems.at[u, phase, k]).wait()
                total = total + came[...].astype(F32)
        dim = ORDERS[group][phase + 1]
        if phase == 0:
            sums[u][...] = total.astype(BF)
            for step in (2, 1, 3):
                index = rows_at(1, group, (at[dim] + step) % 4)
                remote(
                    sums[u].at[index], got[u][1].at[step - 1], send_sems.at[u, 1, step - 1],
                    recv_sems.at[u, 1, step - 1], device_at(moved(at, dim, step)),
                )
            return
        parts[u][...] = total.reshape(SUMMED[group][1] + (2, 8, width_of(UNITS[u])))
        for step in (2, 1, 3, 0):
            index = rows_at(2, group, (at[dim] + step) % 4)
            there = moved(at, dim, step)
            for flip in (0, 1):
                if step or flip:
                    to = moved(there, "core", flip)
                    remote(
                        parts[u].at[index + (to["core"],)], last[u].at[core * 4 + step],
                        final_sems.at[0, u, 2 * step + flip], final_sems.at[1, u, 0], device_at(to),
                    )
        index = rows_at(2, group, at[dim])
        last[u][core * 4] = parts[u][index + (core,)]

    def finish(u):
        most = pl.ds(0, 7)
        pltpu.make_async_copy(last[u].at[most], last[u].at[most], final_sems.at[1, u, 0]).wait()
        for half in range(2):
            total = last[u][4 * half]
            for k in range(1, 4):
                total = total + last[u][4 * half + k]
            total = total * scale
            col = 0
            for which, block, first, width in SHARES[UNITS[u]]:
                target, start = (out_ref, 0) if which else (in_ref, block * 2 * HALF)
                cols = slice(start + half * HALF + first, start + half * HALF + first + width)
                target[:, cols] = total[:, col : col + width]
                col += width

    def add_in_grad(grad, block):
        for j in range(4):
            part = lax.dot_general(
                grad[...], weights[block, columns(j), :], NT, preferred_element_type=F32
            )
            grad_in[:, columns(j)] = part if block == 2 else grad_in[:, columns(j)] + part

    pairs = [
        pair_up(4, block_in, left_peer.at[0]),
        pair_up(5, second_out, left_peer.at[1]),
        pair_right(2),
        pair_right(3),
    ]
    shape = (2, 4, 4, 2, 16, 128)
    for k, ref in enumerate((block_in, second_out)):
        left[k, :, :, :, :, :, :128] = ref[...].T.reshape(shape)
    for copy in pairs:
        copy.wait_recv()
    for k in range(2):
        left[k, :, :, :, :, :, 128:] = left_peer[k].T.reshape(shape)
    for u in range(3):
        start_unit(u)
    if EARLY:
        for u in range(3):
            send_unit(u)
    add_in_grad(gate_two_grad, 2)

    def receive(k):
        wait_wave(pieces_out.at[k], pieces_in.at[k], wave_recv.at[k], wave_own.at[k])
        wide[k] = pieces_in[k].astype(F32).reshape(DEV * WAVE, LANES)

    def pull(field, c):
        start = field % 2 * CH + c
        return jnp.concatenate(
            [wide[field // 2, pl.ds(start + h, DEV, WAVE), :] for h in range(2)], axis=1
        )

    def push(field, c, data):
        for h in range(2):
            narrow[field // 2, pl.ds(field % 2 * CH + c + h, DEV, WAVE), :] = data[
                :, h * 128 : h * 128 + 128
            ]

    def first(i, carry):
        c = 2 * i
        gate, conv = pull(GATE_ONE, c), pull(CONV_ONE, c)
        first_out = round_mul(gate, conv)
        grad_first, filter_two_part = correlations(
            pull(GRAD_CONV_TWO, c),
            jnp.concatenate([pull(FILTER_TWO, c), first_out], axis=0),
            refs,
            factor,
        )
        push(GRAD_GATE_ONE, c, round_mul(grad_first, conv))
        push(FILTER_TWO_GRAD, c, filter_two_part)
        gate_one_all[i] = round_mul(grad_first, gate)
        return carry

    def second(i, carry):
        c = 2 * i
        grad_value, filter_one_part = correlations(
            gate_one_all[i],
            jnp.concatenate([pull(FILTER_ONE, c), pull(VALUE, c)], axis=0),
            refs,
            factor,
        )
        push(GRAD_VALUE, c, grad_value)
        push(FILTER_ONE_GRAD, c, filter_one_part)
        return carry

    def send_back(k):
        backs_out[k] = narrow[k].astype(BF).reshape(DEV, WAVE, LANES)
        send(3 + k, backs_out.at[k], backs_in.at[k])

    def wait_back(k):
        wait_wave(backs_out.at[k], backs_in.at[k], wave_recv.at[3 + k], wave_own.at[3 + k])

    def take_back(field, result):
        start = field % 2 * CH
        for j in range(4):
            part = backs_in[field // 2, pl.ds(32 * j, 32)].astype(F32)[:, start : start + CH]
            result[:, columns(j)] = part.reshape(256, LANES).T.astype(BF)

    receive(0)
    receive(1)
    if not EARLY:
        for u in range(3):
            send_unit(u)
    lax.fori_loop(0, CH // 2, first, 0, unroll=UNROLL)
    send_back(0)
    for u in range(min(3, RINGS)):
        pass_on(u)
    receive(2)
    lax.fori_loop(0, CH // 2, second, 0, unroll=UNROLL)
    send_back(1)
    wait_back(0)
    take_back(GRAD_GATE_ONE, gate_one_grad)
    pair_right(1).wait_recv()
    for u in range(3, 6):
        start_unit(u)
        send_unit(u)
    add_in_grad(gate_one_grad, 1)
    for u in range(3):
        advance(u, 0)
    wait_back(1)
    take_back(GRAD_VALUE, value_grad)
    pair_right(0).wait_recv()
    for u in range(6, 9):
        start_unit(u)
        send_unit(u)
    for u in range(3, min(6, RINGS)):
        pass_on(u)
    for u in range(3):
        advance(u, 1)
    add_in_grad(value_grad, 0)
    in_grad[...] = grad_in[...].astype(BF)
    for u in range(3, 6):
        advance(u, 0)
    for u in range(6, RINGS):
        pass_on(u)
    for u in range(6, 9):
        advance(u, 0)
    for u in range(3, 6):
        advance(u, 1)
    for u in range(3):
        finish(u)
    take_back(FILTER_TWO_GRAD, filter_two_grad)
    for u in range(6, 9):
        advance(u, 1)
    for u in range(3, 6):
        finish(u)
    take_back(FILTER_ONE_GRAD, filter_one_grad)
    for u in range(6, 9):
        finish(u)
    for k in range(3):
        wait_wave(pieces_out.at[k], pieces_in.at[k], wave_send.at[k])
    for k in range(2):
        wait_wave(backs_out.at[k], backs_in.at[k], wave_send.at[3 + k])
    for copy in copies:
        copy.wait_send()


def store_kernel(*refs):
    for src, dst in zip(refs[:5], refs[5:]):
        dst[...] = src[...]


def shards(block_in, out_cot, w_in, w_out, conv_one, conv_two, filter_one, filter_two):
    rows, width = block_in.shape
    seq_len = rows * DEV
    scale = seq_len ** (-0.5)
    factor = scale / (2.0 * seq_len)
    tables = [jnp.asarray(t) for t in dft_tables()]
    own, got, sums, parts, last = [], [], [], [], []
    for unit in UNITS:
        w = width_of(unit)
        first, second, _ = SUMMED[unit[1]]
        own.append(pltpu.VMEM((4,) + first + (16, w), BF))
        got.append([pltpu.VMEM((3,) + shape + (16, w), BF) for shape in (first, second)])
        sums.append(pltpu.VMEM(first + (16, w), BF))
        parts.append(pltpu.VMEM(second + (2, 8, w), F32))
        last.append(pltpu.VMEM((8, 8, w), F32))
    vmem = pl.BlockSpec(memory_space=pltpu.VMEM)
    anywhere = pl.BlockSpec(memory_space=pl.ANY)
    wave = (DEV, WAVE, LANES)
    flat = (DEV * WAVE, LANES)
    local = jax.ShapeDtypeStruct((rows, width), BF)
    dma = pltpu.SemaphoreType.DMA
    units = len(UNITS)
    outputs = (
        local,
        jax.ShapeDtypeStruct((width // DEV, 3 * width), F32),
        jax.ShapeDtypeStruct((width // DEV, width), F32),
        local,
        local,
    )
    results = pl.pallas_call(
        functools.partial(kernel, factor, scale),
        out_shape=outputs,
        in_specs=[vmem] * 6 + [anywhere] * 2 + [vmem] * 5,
        out_specs=(vmem,) * 5,
        scratch_shapes=[
            pltpu.VMEM((4, width, width), BF),
            pltpu.VMEM((rows, width), F32),
            pltpu.VMEM((rows, width), BF),
            pltpu.VMEM((rows, width), BF),
            pltpu.VMEM((rows, width), BF),
            pltpu.VMEM((rows, width), BF),
            pltpu.VMEM((CH // 2, DEV, 256), F32),
            pltpu.VMEM((3,) + wave, BF),
            pltpu.VMEM((3,) + wave, BF),
            pltpu.VMEM((2,) + wave, BF),
            pltpu.VMEM((2,) + wave, BF),
            pltpu.VMEM((3,) + flat, F32),
            pltpu.VMEM((2,) + flat, F32),
            pltpu.VMEM((2, 2, 4, 4, 2, 16, 256), BF),
            pltpu.VMEM((2, rows, width), BF),
            pltpu.VMEM((4, rows, HALF), BF),
            own, got, sums, parts, last,
            dma((4,)),
            dma((5,)),
            dma((5,)),
            dma((5,)),
            dma((2, 6)),
            dma((units, 2, 6)),
            dma((units, 2, 6)),
            dma((2, units, 8)),
            pltpu.SemaphoreType.REGULAR((1,)),
        ],
        compiler_params=pltpu.CompilerParams(
            vmem_limit_bytes=60 << 20, collective_id=0, has_side_effects=True
        ),
        name="hyena_backward",
    )(block_in, out_cot, conv_one, conv_two, filter_one, filter_two, w_in, w_out, *tables)
    return pl.pallas_call(
        store_kernel,
        out_shape=outputs,
        in_specs=[vmem] * 5,
        out_specs=(vmem,) * 5,
        name="store",
    )(*results)


def solution(mesh):
    rows = P(AXES, None)
    return jax.shard_map(
        shards,
        mesh=mesh,
        in_specs=(rows, rows, P(), P(), rows, rows, rows, rows),
        out_specs=(rows,) * 5,
        check_vma=False,
    )
```

```python
import functools

import jax
import jax.numpy as jnp
import numpy as np
from jax import lax
from jax.experimental import pallas as pl
from jax.experimental.pallas import tpu as pltpu
from jax.sharding import PartitionSpec as P

AXES = ("major", "minor")
DEV = 128
CH = 8
LANES = 128
BF = jnp.bfloat16
F32 = jnp.float32
CONV_ONE, FILTER_TWO, GATE_ONE, GRAD_CONV_TWO, FILTER_ONE, VALUE = range(6)
GRAD_GATE_ONE, FILTER_TWO_GRAD, GRAD_VALUE, FILTER_ONE_GRAD = range(4)
FIELDS_IN = 6
EARLY = True
UNROLL = 2
RINGS = 6
FIRST_AFTER = 2
NEAR_AFTER = 0
FIELDS_OUT = 4
WAVE = 2 * CH
MESH = pl.DeviceIdType.MESH


def dft_tables():
    k1 = np.arange(256)[:, None]
    n1 = np.arange(128)[None, :]
    a = 2.0 * np.pi * ((k1 * n1) % 256) / 256
    c, s = np.cos(a), np.sin(a)
    n2 = np.arange(128)
    b = 2.0 * np.pi * ((n2[:, None] * n2[None, :]) % 128) / 128
    cb, sb = np.cos(b), np.sin(b)
    t = 2.0 * np.pi * (k1 * n2[None, :]) / 32768
    return (
        np.block([[c, -s], [-s, -c]]).astype(BF),
        np.block([[c.T, -s.T], [s.T, c.T]]).astype(BF),
        np.block([[cb, -sb], [sb, cb]]).astype(BF),
        np.block([[cb, sb], [-sb, cb]]).astype(BF),
        np.stack([np.cos(t), np.sin(t)]).astype(np.float32),
    )


def round_mul(a, b):
    return (a * b).astype(BF).astype(F32)


def spectrum_of(data, table, line, tw_re, tw_im):
    grid = jnp.dot(table, data, preferred_element_type=F32)
    out = []
    for h in range(2):
        re = grid[:256, h * 128 : h * 128 + 128]
        im = grid[256:, h * 128 : h * 128 + 128]
        turned = jnp.concatenate([re * tw_re + im * tw_im, im * tw_re - re * tw_im], axis=1)
        out.append(jnp.dot(turned.astype(BF), line, preferred_element_type=F32))
    return out


def correlations(left, pair, refs, factor):
    fwd, inv, line, line_back, turn = refs
    tw_re, tw_im = turn[0], turn[1]
    specs = spectrum_of(left.astype(BF), fwd[:, :128], line[...], tw_re, tw_im)
    packs = spectrum_of(pair.astype(BF), fwd[...], line[...], tw_re, tw_im)
    backs_re, backs_im = [], []
    for spec, pack in zip(specs, packs):
        l_re, l_im = spec[:, :128], spec[:, 128:]
        p_re, p_im = pack[:, :128], pack[:, 128:]
        both = jnp.concatenate([l_re * p_re + l_im * p_im, l_im * p_re - l_re * p_im], axis=1)
        back = jnp.dot(both.astype(BF), line_back[...], preferred_element_type=F32)
        b_re, b_im = back[:, :128], back[:, 128:]
        backs_re.append(b_re * tw_re - b_im * tw_im)
        backs_im.append(b_re * tw_im + b_im * tw_re)
    stacked = jnp.concatenate(
        [jnp.concatenate(backs_re, axis=1), jnp.concatenate(backs_im, axis=1)], axis=0
    ).astype(BF)
    out = jnp.dot(inv[...], stacked, preferred_element_type=F32) * factor
    return out[:128].astype(BF).astype(F32), out[128:].astype(BF).astype(F32)


def peer_of(step):
    rem, div = lax.rem, lax.div
    step = rem(step * 37, DEV)
    major, minor = lax.axis_index("major"), lax.axis_index("minor")
    x = rem(rem(div(minor, 2), 2) * 2 + div(major, 4) + div(step, 2), 4)
    y = rem(rem(major, 4) + div(step, 8), 4)
    z = rem(div(minor, 4) + div(step, 32), 4)
    core = rem(minor + step, 2)
    return (rem(x, 2) * 4 + y, z * 4 + div(x, 2) * 2 + core)


def my_index():
    return lax.axis_index("major") * 16 + lax.axis_index("minor")


def send_wave(src, dst, send_sem, recv_sem, own_sem):
    me = my_index()
    pltpu.make_async_copy(src.at[me], dst.at[me], own_sem).start()

    def send(step, carry):
        major, minor = peer_of(step)
        pltpu.make_async_remote_copy(
            src_ref=src.at[major * 16 + minor],
            dst_ref=dst.at[me],
            send_sem=send_sem,
            recv_sem=recv_sem,
            device_id=(major, minor),
            device_id_type=MESH,
        ).start()
        return carry

    lax.fori_loop(1, DEV, send, 0)


def wait_wave(src, dst, sem, own_sem=None):
    if own_sem is not None:
        me = my_index()
        pltpu.make_async_copy(src.at[me], dst.at[me], own_sem).wait()
    most = pl.ds(0, DEV - 1)
    pltpu.make_async_copy(src.at[most], dst.at[most], sem).wait()


HALF = 512
SHARES = {
    (0, 0): [(0, 2, 0, 256), (1, 3, 0, 128)],
    (0, 1): [(0, 2, 256, 128), (1, 3, 128, 256)],
    (0, 2): [(0, 2, 384, 128), (1, 3, 384, 128)],
    (1, 0): [(0, 1, 0, 128)],
    (1, 1): [(0, 1, 128, 128)],
    (1, 2): [(0, 1, 256, 256)],
    (2, 0): [(0, 0, 0, 256)],
    (2, 1): [(0, 0, 256, 128)],
    (2, 2): [(0, 0, 384, 128)],
}
ORDERS = (("y", "z", "x"), ("z", "x", "y"), ("x", "y", "z"))
UNITS = [(w, g) for w in range(3) for g in range(3)]


def width_of(unit):
    return sum(share[3] for share in SHARES[unit])


def coordinates():
    major, minor = lax.axis_index("major"), lax.axis_index("minor")
    x = (minor // 2) % 2 * 2 + major // 4
    return {"x": x, "y": major % 4, "z": minor // 4, "core": minor % 2}


def device_at(at):
    return (at["x"] % 2 * 4 + at["y"], at["z"] * 4 + at["x"] // 2 * 2 + at["core"])


def moved(at, dim, step):
    return dict(at, **{dim: (at[dim] + step) % (2 if dim == "core" else 4)})


def rows_at(phase, group, value):
    every = slice(None)
    if group == 0:
        return [(every, value), (every, value), (value % 2, value // 2)][phase]
    if group == 1:
        return [(every, every, value), (value % 2, every, value // 2), (value,)][phase]
    return [(value % 2, every, every, value // 2), (value,), (value,)][phase]


SUMMED = (
    ((2, 4, 2), (2, 2), ()),
    ((2, 4, 2), (4,), ()),
    ((4, 4), (4,), ()),
)


NT = (((1,), (1,)), ((), ()))


def product(left, right):
    return (left.astype(F32) * right.astype(F32)).astype(BF)


def kernel(
    factor, scale,
    block_in, out_cot, conv_one, conv_two, filter_one, filter_two, w_in, w_out,
    fwd, inv, line, line_back, turn,
    in_grad, in_ref, out_ref, filter_one_grad, filter_two_grad,
    weights, grad_in, value_grad, gate_one_grad, gate_two_grad, second_out, gate_one_all,
    pieces_out, pieces_in, backs_out, backs_in, wide, narrow,
    left, left_peer, right_peer, own, got, sums, parts, last,
    weight_sems, wave_send, wave_recv, wave_own, pair_sems, send_sems, recv_sems, final_sems,
    greet_sems,
):
    at = coordinates()
    core = at["core"]
    partner = device_at(moved(at, "core", 1))
    refs = (fwd, inv, line, line_back, turn)
    copies = []

    def greet(sem, devices):
        for device in devices:
            pl.semaphore_signal(sem, inc=1, device_id=device, device_id_type=MESH)

    def remote(src, dst, send_sem, recv_sem, device):
        copy = pltpu.make_async_remote_copy(
            src_ref=src, dst_ref=dst, send_sem=send_sem, recv_sem=recv_sem,
            device_id=device, device_id_type=MESH,
        )
        copy.start()
        copies.append(copy)
        return copy

    barrier = pltpu.get_barrier_semaphore()
    line_of = [moved(at, "x", k) for k in range(4)]
    line_of = line_of[1:] + [moved(one, "core", 1) for one in line_of]
    plane = [moved(moved(at, "y", j), "z", k) for j in range(4) for k in range(4) if j or k]
    plane = [device_at(one) for one in plane]
    near = plane + [device_at(one) for one in line_of]
    greet(barrier, near)

    loads = []
    for k in (1, 2, 3, 0):
        src = w_out if k == 3 else w_in.at[:, pl.ds(k * 1024, 1024)]
        loads.append(pltpu.make_async_copy(src, weights.at[k], weight_sems.at[k]))
        loads[-1].start()

    def put_pieces(wave, j, one, two):
        both = [part.astype(F32).T.reshape(32, CH, LANES) for part in (one, two)]
        pieces_out[wave, pl.ds(32 * j, 32)] = jnp.concatenate(both, axis=1).astype(BF)

    def columns(j):
        return slice(256 * j, 256 * j + 256)

    def send(k, src, dst):
        send_wave(src, dst, wave_send.at[k], wave_recv.at[k], wave_own.at[k])

    for j in range(4):
        put_pieces(0, j, conv_one[:, columns(j)], filter_two[:, columns(j)])
    if NEAR_AFTER < 0:
        pl.semaphore_wait(barrier, len(near))
        greet(greet_sems.at[0], plane)
    for load in loads[:3]:
        load.wait()
    for j in range(4):
        c = columns(j)
        gate_one = jnp.dot(block_in[...], weights[1, :, c], preferred_element_type=F32).astype(BF)
        gate_two = jnp.dot(block_in[...], weights[2, :, c], preferred_element_type=F32).astype(BF)
        grad_second = lax.dot_general(
            out_cot[...], weights[3, c, :], NT, preferred_element_type=F32
        ).astype(BF)
        gate_two_grad[:, c] = product(grad_second, conv_two[:, c])
        second_out[:, c] = product(gate_two, conv_two[:, c])
        put_pieces(1, j, gate_one, product(grad_second, gate_two))
        if j == NEAR_AFTER:
            pl.semaphore_wait(barrier, len(near))
            greet(greet_sems.at[0], plane)
        if j == FIRST_AFTER:
            pl.semaphore_wait(greet_sems.at[0], len(plane))
            send(0, pieces_out.at[0], pieces_in.at[0])
    send(1, pieces_out.at[1], pieces_in.at[1])
    loads[3].wait()
    for j in range(4):
        value = jnp.dot(block_in[...], weights[0, :, columns(j)], preferred_element_type=F32)
        put_pieces(2, j, filter_one[:, columns(j)], value.astype(BF))
    send(2, pieces_out.at[2], pieces_in.at[2])

    theirs = pl.ds(pl.multiple_of((1 - core) * HALF, HALF), HALF)
    rights = (value_grad, gate_one_grad, gate_two_grad, out_cot)

    def pair_up(k, src, dst):
        return remote(src, dst, pair_sems.at[0, k], pair_sems.at[1, k], partner)

    def pair_right(block):
        return pair_up(block, rights[block].at[:, theirs], right_peer.at[block])

    def start_unit(u):
        group = UNITS[u][1]
        dim = ORDERS[group][0]
        for step in (2, 1, 3, 0):
            index = rows_at(0, group, (at[dim] + step) % 4)
            col = 0
            for which, block, first, width in SHARES[UNITS[u]]:
                rows = left[(which,) + index].reshape(256, 256)
                cols = pl.ds(pl.multiple_of(core * HALF + first, 128), width)
                right = jnp.concatenate(
                    [rights[block][:, cols], right_peer[block, :, first : first + width]], axis=0
                )
                own[u][step, ..., col : col + width] = (
                    jnp.dot(rows, right, preferred_element_type=F32)
                    .astype(BF)
                    .reshape(SUMMED[group][0] + (16, width))
                )
                col += width

    def halves(u):
        count = SUMMED[UNITS[u][1]][0][0] // 2
        return pl.ds(0, count), pl.ds(count, count)

    def send_unit(u):
        dim = ORDERS[UNITS[u][1]][0]
        if u >= RINGS:
            for step in (2, 1, 3):
                remote(
                    own[u].at[step], got[u][0].at[step - 1], send_sems.at[u, 0, step - 1],
                    recv_sems.at[u, 0, step - 1], device_at(moved(at, dim, step)),
                )
            return
        low, high = halves(u)
        for k, (step, rows, to, slot) in enumerate(
            ((2, low, 1, 1), (2, high, 3, 1), (1, high, 1, 0), (3, low, 3, 2))
        ):
            remote(
                own[u].at[step, rows], got[u][0].at[slot, rows], send_sems.at[u, 0, k],
                recv_sems.at[u, 0, k], device_at(moved(at, dim, to)),
            )

    def pass_on(u):
        dim = ORDERS[UNITS[u][1]][0]
        low, high = halves(u)
        for k, (step, rows) in enumerate(((1, low), (3, high))):
            came = got[u][0].at[1, rows]
            pltpu.make_async_copy(came, came, recv_sems.at[u, 0, k]).wait()
            mine = own[u][step, rows].astype(F32) + came[...].astype(F32)
            own[u][step, rows] = mine.astype(BF)
            remote(
                own[u].at[step, rows], got[u][0].at[step - 1, rows], send_sems.at[u, 0, 4 + k],
                recv_sems.at[u, 0, 4 + k], device_at(moved(at, dim, step)),
            )

    def advance(u, phase):
        group = UNITS[u][1]
        base = own[u].at[0] if phase == 0 else sums[u]
        index = () if phase == 0 else rows_at(phase, group, at[ORDERS[group][phase]])
        total = base[index + (Ellipsis,)].astype(F32)
        if phase == 0 and u < RINGS:
            low, high = halves(u)
            for k, slot, rows in ((2, 0, high), (3, 2, low), (4, 0, low), (5, 2, high)):
                came = got[u][0].at[slot, rows]
                pltpu.make_async_copy(came, came, recv_sems.at[u, 0, k]).wait()
            total = total + got[u][0][0].astype(F32) + got[u][0][2].astype(F32)
        else:
            for k in range(3):
                came = got[u][phase].at[k]
                pltpu.make_async_copy(came, came, recv_sems.at[u, phase, k]).wait()
                total = total + came[...].astype(F32)
        dim = ORDERS[group][phase + 1]
        if phase == 0:
            sums[u][...] = total.astype(BF)
            for step in (2, 1, 3):
                index = rows_at(1, group, (at[dim] + step) % 4)
                remote(
                    sums[u].at[index], got[u][1].at[step - 1], send_sems.at[u, 1, step - 1],
                    recv_sems.at[u, 1, step - 1], device_at(moved(at, dim, step)),
                )
            return
        parts[u][...] = total.reshape(SUMMED[group][1] + (2, 8, width_of(UNITS[u])))
        for step in (2, 1, 3, 0):
            index = rows_at(2, group, (at[dim] + step) % 4)
            there = moved(at, dim, step)
            for flip in (0, 1):
                if step or flip:
                    to = moved(there, "core", flip)
                    remote(
                        parts[u].at[index + (to["core"],)], last[u].at[core * 4 + step],
                        final_sems.at[0, u, 2 * step + flip], final_sems.at[1, u, 0], device_at(to),
                    )
        index = rows_at(2, group, at[dim])
        last[u][core * 4] = parts[u][index + (core,)]

    def finish(u):
        most = pl.ds(0, 7)
        pltpu.make_async_copy(last[u].at[most], last[u].at[most], final_sems.at[1, u, 0]).wait()
        for half in range(2):
            total = last[u][4 * half]
            for k in range(1, 4):
                total = total + last[u][4 * half + k]
            total = total * scale
            col = 0
            for which, block, first, width in SHARES[UNITS[u]]:
                target, start = (out_ref, 0) if which else (in_ref, block * 2 * HALF)
                cols = slice(start + half * HALF + first, start + half * HALF + first + width)
                target[:, cols] = total[:, col : col + width]
                col += width

    def add_in_grad(grad, block):
        for j in range(4):
            part = lax.dot_general(
                grad[...], weights[block, columns(j), :], NT, preferred_element_type=F32
            )
            grad_in[:, columns(j)] = part if block == 2 else grad_in[:, columns(j)] + part

    pairs = [
        pair_up(4, block_in, left_peer.at[0]),
        pair_up(5, second_out, left_peer.at[1]),
        pair_right(2),
        pair_right(3),
    ]
    shape = (2, 4, 4, 2, 16, 128)
    for k, ref in enumerate((block_in, second_out)):
        left[k, :, :, :, :, :, :128] = ref[...].T.reshape(shape)
    for copy in pairs:
        copy.wait_recv()
    for k in range(2):
        left[k, :, :, :, :, :, 128:] = left_peer[k].T.reshape(shape)
    for u in range(3):
        start_unit(u)
    if EARLY:
        for u in range(3):
            send_unit(u)
    add_in_grad(gate_two_grad, 2)

    def receive(k):
        wait_wave(pieces_out.at[k], pieces_in.at[k], wave_recv.at[k], wave_own.at[k])
        wide[k] = pieces_in[k].astype(F32).reshape(DEV * WAVE, LANES)

    def pull(field, c):
        start = field % 2 * CH + c
        return jnp.concatenate(
            [wide[field // 2, pl.ds(start + h, DEV, WAVE), :] for h in range(2)], axis=1
        )

    def push(field, c, data):
        for h in range(2):
            narrow[field // 2, pl.ds(field % 2 * CH + c + h, DEV, WAVE), :] = data[
                :, h * 128 : h * 128 + 128
            ]

    def first(i, carry):
        c = 2 * i
        gate, conv = pull(GATE_ONE, c), pull(CONV_ONE, c)
        first_out = round_mul(gate, conv)
        grad_first, filter_two_part = correlations(
            pull(GRAD_CONV_TWO, c),
            jnp.concatenate([pull(FILTER_TWO, c), first_out], axis=0),
            refs,
            factor,
        )
        push(GRAD_GATE_ONE, c, round_mul(grad_first, conv))
        push(FILTER_TWO_GRAD, c, filter_two_part)
        gate_one_all[i] = round_mul(grad_first, gate)
        return carry

    def second(i, carry):
        c = 2 * i
        grad_value, filter_one_part = correlations(
            gate_one_all[i],
            jnp.concatenate([pull(FILTER_ONE, c), pull(VALUE, c)], axis=0),
            refs,
            factor,
        )
        push(GRAD_VALUE, c, grad_value)
        push(FILTER_ONE_GRAD, c, filter_one_part)
        return carry

    def send_back(k):
        backs_out[k] = narrow[k].astype(BF).reshape(DEV, WAVE, LANES)
        send(3 + k, backs_out.at[k], backs_in.at[k])

    def wait_back(k):
        wait_wave(backs_out.at[k], backs_in.at[k], wave_recv.at[3 + k], wave_own.at[3 + k])

    def take_back(field, result):
        start = field % 2 * CH
        for j in range(4):
            part = backs_in[field // 2, pl.ds(32 * j, 32)].astype(F32)[:, start : start + CH]
            result[:, columns(j)] = part.reshape(256, LANES).T.astype(BF)

    receive(0)
    receive(1)
    if not EARLY:
        for u in range(3):
            send_unit(u)
    lax.fori_loop(0, CH // 2, first, 0, unroll=UNROLL)
    send_back(0)
    for u in range(min(3, RINGS)):
        pass_on(u)
    receive(2)
    lax.fori_loop(0, CH // 2, second, 0, unroll=UNROLL)
    send_back(1)
    wait_back(0)
    take_back(GRAD_GATE_ONE, gate_one_grad)
    pair_right(1).wait_recv()
    for u in range(3, 6):
        start_unit(u)
        send_unit(u)
    add_in_grad(gate_one_grad, 1)
    wait_back(1)
    take_back(GRAD_VALUE, value_grad)
    pair_right(0).wait_recv()
    for u in range(6, 9):
        start_unit(u)
        send_unit(u)
    for u in range(3, min(6, RINGS)):
        pass_on(u)
    for u in range(3):
        advance(u, 0)
    for u in range(3):
        advance(u, 1)
    add_in_grad(value_grad, 0)
    in_grad[...] = grad_in[...].astype(BF)
    for u in range(3, 6):
        advance(u, 0)
    for u in range(6, RINGS):
        pass_on(u)
    for u in range(6, 9):
        advance(u, 0)
    for u in range(3, 6):
        advance(u, 1)
    for u in range(3):
        finish(u)
    take_back(FILTER_TWO_GRAD, filter_two_grad)
    for u in range(6, 9):
        advance(u, 1)
    for u in range(3, 6):
        finish(u)
    take_back(FILTER_ONE_GRAD, filter_one_grad)
    for u in range(6, 9):
        finish(u)
    for k in range(3):
        wait_wave(pieces_out.at[k], pieces_in.at[k], wave_send.at[k])
    for k in range(2):
        wait_wave(backs_out.at[k], backs_in.at[k], wave_send.at[3 + k])
    for copy in copies:
        copy.wait_send()


def store_kernel(*refs):
    for src, dst in zip(refs[:5], refs[5:]):
        dst[...] = src[...]


def shards(block_in, out_cot, w_in, w_out, conv_one, conv_two, filter_one, filter_two):
    rows, width = block_in.shape
    seq_len = rows * DEV
    scale = seq_len ** (-0.5)
    factor = scale / (2.0 * seq_len)
    tables = [jnp.asarray(t) for t in dft_tables()]
    own, got, sums, parts, last = [], [], [], [], []
    for unit in UNITS:
        w = width_of(unit)
        first, second, _ = SUMMED[unit[1]]
        own.append(pltpu.VMEM((4,) + first + (16, w), BF))
        got.append([pltpu.VMEM((3,) + shape + (16, w), BF) for shape in (first, second)])
        sums.append(pltpu.VMEM(first + (16, w), BF))
        parts.append(pltpu.VMEM(second + (2, 8, w), F32))
        last.append(pltpu.VMEM((8, 8, w), F32))
    vmem = pl.BlockSpec(memory_space=pltpu.VMEM)
    anywhere = pl.BlockSpec(memory_space=pl.ANY)
    wave = (DEV, WAVE, LANES)
    flat = (DEV * WAVE, LANES)
    local = jax.ShapeDtypeStruct((rows, width), BF)
    dma = pltpu.SemaphoreType.DMA
    units = len(UNITS)
    outputs = (
        local,
        jax.ShapeDtypeStruct((width // DEV, 3 * width), F32),
        jax.ShapeDtypeStruct((width // DEV, width), F32),
        local,
        local,
    )
    results = pl.pallas_call(
        functools.partial(kernel, factor, scale),
        out_shape=outputs,
        in_specs=[vmem] * 6 + [anywhere] * 2 + [vmem] * 5,
        out_specs=(vmem,) * 5,
        scratch_shapes=[
            pltpu.VMEM((4, width, width), BF),
            pltpu.VMEM((rows, width), F32),
            pltpu.VMEM((rows, width), BF),
            pltpu.VMEM((rows, width), BF),
            pltpu.VMEM((rows, width), BF),
            pltpu.VMEM((rows, width), BF),
            pltpu.VMEM((CH // 2, DEV, 256), F32),
            pltpu.VMEM((3,) + wave, BF),
            pltpu.VMEM((3,) + wave, BF),
            pltpu.VMEM((2,) + wave, BF),
            pltpu.VMEM((2,) + wave, BF),
            pltpu.VMEM((3,) + flat, F32),
            pltpu.VMEM((2,) + flat, F32),
            pltpu.VMEM((2, 2, 4, 4, 2, 16, 256), BF),
            pltpu.VMEM((2, rows, width), BF),
            pltpu.VMEM((4, rows, HALF), BF),
            own, got, sums, parts, last,
            dma((4,)),
            dma((5,)),
            dma((5,)),
            dma((5,)),
            dma((2, 6)),
            dma((units, 2, 6)),
            dma((units, 2, 6)),
            dma((2, units, 8)),
            pltpu.SemaphoreType.REGULAR((1,)),
        ],
        compiler_params=pltpu.CompilerParams(
            vmem_limit_bytes=60 << 20, collective_id=0, has_side_effects=True
        ),
        name="hyena_backward",
    )(block_in, out_cot, conv_one, conv_two, filter_one, filter_two, w_in, w_out, *tables)
    return pl.pallas_call(
        store_kernel,
        out_shape=outputs,
        in_specs=[vmem] * 5,
        out_specs=(vmem,) * 5,
        name="store",
    )(*results)


def solution(mesh):
    rows = P(AXES, None)
    return jax.shard_map(
        shards,
        mesh=mesh,
        in_specs=(rows, rows, P(), P(), rows, rows, rows, rows),
        out_specs=(rows,) * 5,
        check_vma=False,
    )
```
